32 devices in a mesh: layer: 8 (over z, y), rep: 4 (over x, core).
Axes of the slice: x: 2, y: 2, z: 4, core: 2. Of those that a mesh axis runs over, the one named last changes fastest.
Arguments:
- features: bfloat16 [4096, 128], P('layer'), may hold values from -6 to 6
- weight: bfloat16 [128, 256], replicated, may hold values from -0.5 to 0.5
- out_bias: float32 [256], replicated, may hold values from -3 to 3
- tile_values: bfloat16 [8, 8, 2, 128, 128], P('layer', 'rep'), may hold values from -0.375 to 0.375
- tile_rows: int32 [8, 8, 2], P('layer', 'rep'), may hold values from 0 to 3
- tile_cols: int32 [8, 8, 2], P('layer', 'rep'), may hold values from 0 to 3
- tile_counts: int32 [8, 8, 2], P('layer', 'rep'), may hold values from 0 to 128
- cotangent: bfloat16 [4096, 256], P('layer'), may hold values from -18 to 18
Outputs:
- activation: bfloat16 [4096, 256], P('layer')
- grad_features: bfloat16 [4096, 128], P('layer')
- grad_weight: float32 [128, 256], replicated
- grad_bias: float32 [256], replicated
The draws below stay inside these ranges and needn't reach their ends.
All inputs are finite; a program needn't handle non-finite values.
Results may differ from the reference program's by a relative error of at most 0.0059.
Values may be sent and summed in bfloat16 or wider, within the bound.
A program may use at most 64 MiB of HBM per device.

```python
import math
import jax
import jax.numpy as jnp
from jax import lax

F_IN = 128
HID = 256
TILE = 128
NODE_DEV = 512
SLOTS = 2
NODES = 4096
N_LAYER = 8


def draw_cotangent(key, part):
    row_scale = 1.0 + 2.0 * jnp.arange(NODES, dtype=jnp.float32)[:, None] / (NODES - 1)
    normal_part = jax.random.normal(jax.random.fold_in(key, 3), (NODES, HID), jnp.float32)
    values = jnp.clip(normal_part, -5.0, 5.0) * row_scale
    return values.astype(jnp.bfloat16)


def with_ends(result, own_key, low, largest):
    place = [jax.random.randint(jax.random.fold_in(own_key, axis), (), 0, length) for axis, length in enumerate(result.shape)]
    main_axis = result.shape.index(max(result.shape))
    beside = place[:main_axis] + [(place[main_axis] + 1) % result.shape[main_axis]] + place[main_axis + 1:]
    return result.at[tuple(place)].set(low).at[tuple(beside)].set(largest)


def block_scale(key, extent, shards, smallest, top_value):
    level, own = 1.0, jax.random.fold_in(key, 6)
    for axis_at, blocks in shards:
        draws = jnp.exp(jax.random.uniform(jax.random.fold_in(own, axis_at), (blocks,), jnp.float32, smallest / len(shards), top_value / len(shards)))
        level = level * jnp.repeat(draws, extent[axis_at] // blocks).reshape([-1 if axis == axis_at else 1 for axis in range(len(extent))])
    return level


def scatter_about(own_key, shape, spread, limit, pieces=(), kind=jnp.bfloat16):
    array = jax.random.normal(own_key, shape, jnp.float32) * spread
    if len(pieces) > 0:
        array = block_scale(own_key, shape, pieces, -0.22, 0.18) * array
    return jnp.clip(array, min=-limit, max=limit).astype(kind)


def setup_inputs(seed: int = 0) -> dict:
    streams_of = jax.random.split(jax.random.key(seed), 9)
    features = scatter_about(streams_of[0], (NODES, F_IN), 1.0, 6.0, ((0, 8),))
    weight = scatter_about(streams_of[1], (F_IN, HID), F_IN ** -0.5, 0.5)
    out_bias = scatter_about(streams_of[2], (HID,), 0.5, 3.0, (), jnp.float32)
    tile_values = scatter_about(streams_of[3], (N_LAYER, N_LAYER, SLOTS, TILE, TILE), (N_LAYER * SLOTS * TILE * TILE // (2 * NODE_DEV)) ** -0.5, 0.375, ((0, 8), (1, 4)))
    tile_rows = with_ends(jax.random.randint(streams_of[4], (N_LAYER, N_LAYER, SLOTS), 0, NODE_DEV // TILE), jax.random.fold_in(streams_of[4], 1), 0, (NODE_DEV // TILE) - 1).astype(jnp.int32)
    tile_cols = with_ends(jax.random.randint(streams_of[5], (N_LAYER, N_LAYER, SLOTS), 0, NODE_DEV // TILE), jax.random.fold_in(streams_of[5], 1), 0, (NODE_DEV // TILE) - 1).astype(jnp.int32)
    tile_counts = with_ends(jax.random.randint(streams_of[6], (N_LAYER, N_LAYER, SLOTS), 0, TILE + 1), jax.random.fold_in(streams_of[6], 1), 0, TILE).astype(jnp.int32)
    cotangent = draw_cotangent(jax.random.fold_in(streams_of[8], 71), 0)
    return {"features": features, "weight": weight, "out_bias": out_bias, "tile_values": tile_values, "tile_rows": tile_rows, "tile_cols": tile_cols, "tile_counts": tile_counts, "cotangent": cotangent}


def live_tiles(tile_values, tile_counts, lane_ids):
    return jnp.where(lane_ids < tile_counts[..., None, None], tile_values, jnp.zeros((), tile_values.dtype)).astype(jnp.float32)

def reference(features, weight, out_bias, tile_values, tile_rows, tile_cols, tile_counts, cotangent):
    node_count = features.shape[0]
    row_tiles = NODE_DEV // TILE
    tile_count = node_count // TILE
    lane_ids = jnp.arange(TILE, dtype=jnp.int32)
    section_ids = jnp.arange(N_LAYER, dtype=jnp.int32)
    row_range = jnp.arange(row_tiles, dtype=jnp.int32)
    projected = jnp.dot(features, weight, preferred_element_type=jnp.float32).astype(jnp.bfloat16)
    proj_tiles = projected.reshape(tile_count, TILE, HID)

    def forward_block(block_index):
        tiles_here = live_tiles(tile_values[block_index], tile_counts[block_index], lane_ids)
        columns = (section_ids[:, None] * row_tiles + tile_cols[block_index]).astype(jnp.int32)
        picked = proj_tiles[columns].astype(jnp.float32)
        products = jnp.einsum('skij,skjf->skif', tiles_here, picked, precision=lax.Precision.HIGHEST)
        placer = (tile_rows[block_index][..., None] == row_range).astype(jnp.float32)
        return jnp.einsum('skr,skif->rif', placer, products, precision=lax.Precision.HIGHEST)
    aggregate = lax.map(forward_block, section_ids).reshape(node_count, HID)
    pre_act = projected.astype(jnp.float32) + aggregate + out_bias.astype(jnp.float32)
    sigmoid_part = jax.nn.sigmoid(pre_act)
    activation = (pre_act * sigmoid_part).astype(jnp.bfloat16)
    grad_pre = (cotangent.astype(jnp.float32) * sigmoid_part * (1.0 + pre_act * (1.0 - sigmoid_part))).astype(jnp.bfloat16)
    grad_tiles = grad_pre.reshape(tile_count, TILE, HID)

    def backward_block(running, block_index):
        tiles_here = live_tiles(tile_values[block_index], tile_counts[block_index], lane_ids)
        sources = (block_index * row_tiles + tile_rows[block_index]).astype(jnp.int32)
        picked = grad_tiles[sources].astype(jnp.float32)
        products = jnp.einsum('skij,skif->skjf', tiles_here, picked, precision=lax.Precision.HIGHEST)
        columns = (section_ids[:, None] * row_tiles + tile_cols[block_index]).astype(jnp.int32)
        running = running.at[columns.reshape(-1)].add(products.reshape(-1, TILE, HID))
        return (running, None)
    start_sum = jnp.zeros((tile_count, TILE, HID), jnp.float32)
    transposed, _ = lax.scan(backward_block, start_sum, section_ids)
    grad_projected = (grad_pre.astype(jnp.float32) + transposed.reshape(node_count, HID)).astype(jnp.bfloat16)
    grad_features = jnp.dot(grad_projected, weight.T, preferred_element_type=jnp.float32).astype(jnp.bfloat16)
    grad_scale = 1.0 / math.sqrt(node_count)
    grad_weight = jnp.dot(features.T, grad_projected, preferred_element_type=jnp.float32) * grad_scale
    grad_bias = lax.optimization_barrier(jnp.sum(grad_pre.astype(jnp.float32), axis=0)) * grad_scale
    return (activation, grad_features, grad_weight, grad_bias)
```

```python
import functools
import math

import jax
import jax.numpy as jnp
from jax import lax
from jax.experimental import pallas as pl
from jax.experimental.pallas import tpu as pltpu
from jax.sharding import PartitionSpec as P

BF = jnp.bfloat16
F32 = jnp.float32
NT = (((1,), (1,)), ((), ()))
NN = (((1,), (0,)), ((), ()))
MESH = pl.DeviceIdType.MESH


def dot(a, b, dims):
    return lax.dot_general(a, b, dims, preferred_element_type=F32)


def kernel(
    L, R, grad_scale,
    feat_h, w_h, bias_h, tv_h, rows_h, cols_h, counts_h, cot_h,
    act_o, gf_o, gw_o, gb_o,
    feat, w, bias, rows, cols, counts, cot, in_sem,
    tiles, xt, yt, wt, biasb, cot_t, act_t, grad, hid, psend, precv, mrecv, wsend, wrecv, wfin, gft,
    t_send, t_fwd, t_recv, x_send, x_fwd, x_recv, y_send, y_recv, m_send, m_recv,
    q_send, q_recv, w_send, w_recv, f_send, f_recv, g_send, g_recv,
):
    l = lax.axis_index("layer")
    r = lax.axis_index("rep")
    tile = tiles.shape[2]
    sections = counts.shape[1]
    slots = counts.shape[2]
    f_in, hidden = w.shape
    fs = f_in // R
    nt = feat.shape[0] // tile
    meta_at = slots * tile
    metas = tiles.shape[1] - meta_at
    twin_l = l + 1 - 2 * lax.rem(l, 2)
    twin_r = r + 1 - 2 * lax.rem(r, 2)

    def remote(src, dst, ssem, rsem, to_l, to_r):
        return pltpu.make_async_remote_copy(
            src_ref=src, dst_ref=dst, send_sem=ssem, recv_sem=rsem,
            device_id={"layer": to_l, "rep": to_r}, device_id_type=MESH,
        )

    def each(n, fn, start=0):
        lax.fori_loop(start, n, lambda i, c: (fn(i), c)[1], 0)

    def groups(n, size, fn, start=0):
        if n <= 8:
            for i in range(start, n, size):
                fn(list(range(i, min(i + size, n))))
        else:
            each(n, lambda i: fn([i]), start)

    barrier = pltpu.get_barrier_semaphore()
    loads = [
        pltpu.make_async_copy(src, dst, in_sem.at[i])
        for i, (src, dst) in enumerate((
            (counts_h, counts), (rows_h, rows), (cols_h, cols), (feat_h, feat),
            (tv_h, tiles.at[pl.ds(r * sections, sections), pl.ds(0, meta_at)]),
            (w_h, w), (bias_h, bias), (cot_h, cot)))
    ]
    for load in loads:
        load.start()

    def greet_layer(d):
        pl.semaphore_signal(
            barrier, inc=1, device_id={"layer": lax.rem(l + d, L), "rep": r}, device_id_type=MESH)

    def greet_rep(d):
        pl.semaphore_signal(
            barrier, inc=1, device_id={"layer": l, "rep": lax.rem(r + d, R)}, device_id_type=MESH)

    each(L, greet_layer, 1)
    each(R, greet_rep, 1)

    for load in loads[:3]:
        load.wait()
    lanes = lax.broadcasted_iota(jnp.int32, (metas, tile), 1)
    row_ids = lax.broadcasted_iota(jnp.int32, (metas, tile), 0)
    for j in range(sections):
        meta = jnp.zeros((metas, tile), F32)
        for k in range(slots):
            base = 2 * nt * k
            meta = meta + jnp.where(row_ids == base + rows[0, j, k], 1.0, 0.0)
            live = jnp.where(lanes < counts[0, j, k], 1.0, 0.0)
            meta = meta + jnp.where(row_ids == base + nt + cols[0, j, k], live, 0.0)
        tiles[r * sections + j, pl.ds(meta_at, metas), :] = meta.astype(BF)

    loads[3].wait()
    pick = (lax.broadcasted_iota(jnp.int32, (fs, f_in), 1)
            == r * fs + lax.broadcasted_iota(jnp.int32, (fs, f_in), 0))
    own = dot(jnp.where(pick, 1.0, 0.0).astype(BF), feat[...], NT).astype(BF)
    for t in range(nt):
        xt[l, pl.ds(t * fs, fs), :] = own[:, t * tile:(t + 1) * tile]
    loads[4].wait()

    pl.semaphore_wait(barrier, L - 1 + R - 1)

    def x_direct(d):
        p = lax.rem(l + 2 * d, L)
        return remote(xt.at[l], xt.at[l], x_send.at[d], x_recv.at[l], p, r)

    def x_forward(d):
        p = lax.rem(l + 2 * d, L)
        return remote(xt.at[p], xt.at[p], x_fwd.at[d], x_recv.at[p], twin_l, r)

    def x_arrival(p):
        return remote(xt.at[p], xt.at[p], x_fwd.at[0], x_recv.at[p], twin_l, r)

    def t_block(q):
        return tiles.at[pl.ds(q * sections, sections)]

    def t_direct(d):
        return remote(t_block(r), t_block(r), t_send.at[d], t_recv.at[r], l, lax.rem(r + 2 * d, R))

    def t_forward(d):
        q = lax.rem(r + 2 * d, R)
        return remote(t_block(q), t_block(q), t_fwd.at[d], t_recv.at[q], l, twin_r)

    def t_arrival(q):
        return remote(t_block(q), t_block(q), t_fwd.at[0], t_recv.at[q], l, twin_r)

    each(R // 2, lambda d: t_direct(d).start(), 1)
    each(L // 2, lambda d: x_direct(L // 2 - d).start(), 1)
    x_forward(0).start()
    t_forward(0).start()

    for load in loads[5:]:
        load.wait()
    wt[...] = jnp.transpose(w[...].astype(F32), (1, 0)).astype(BF)
    biasb[...] = jnp.transpose(jnp.broadcast_to(bias[...], (tile, hidden)), (1, 0))
    for t in range(nt):
        part = cot[pl.ds(t * tile, tile), :].astype(F32)
        cot_t[t] = jnp.transpose(part, (1, 0)).astype(BF)

    def relay_tiles(d):
        t_arrival(lax.rem(r + 2 * d, R)).wait_recv()
        t_forward(d).start()

    def relay_x(d):
        x_arrival(lax.rem(l + 2 * d, L)).wait_recv()
        x_forward(d).start()

    each(R // 2, relay_tiles, 1)
    each(L // 2, relay_x, 1)
    each(R // 2, lambda d: t_arrival(lax.rem(twin_r + 2 * d, R)).wait_recv())

    hid[...] = xt[l].astype(F32)

    def gather_sections(ids):
        sums = [hid[pl.ds(t * fs, fs), :] for t in range(nt)]
        for s in ids:
            meta = tiles[s, pl.ds(meta_at, metas), :].astype(F32)
            blocks = [xt[s, pl.ds(c * fs, fs), :].astype(F32) for c in range(nt)]
            for k in range(slots):
                base = 2 * nt * k
                picked = sum(
                    meta[base + nt + c:base + nt + c + 1, :] * blocks[c] for c in range(nt)
                ).astype(BF)
                product = dot(picked, tiles[s, pl.ds(k * tile, tile), :], NT)
                for t in range(nt):
                    sums[t] = sums[t] + meta[base + t:base + t + 1, :] * product
        for t in range(nt):
            hid[pl.ds(t * fs, fs), :] = sums[t]

    def late_sections(ds):
        ids = [lax.rem(twin_l + 2 * d, L) for d in ds]
        for p in ids:
            x_arrival(p).wait_recv()
        gather_sections(ids)

    groups(L // 2, 4, lambda ds: gather_sections([lax.rem(l + 2 * d, L) for d in ds]))
    groups(L // 2, 2, late_sections)

    yt[r] = hid[...].astype(BF)

    def y_copy(q, d):
        return remote(yt.at[q], yt.at[q], y_send.at[d], y_recv.at[q], l, lax.rem(r + d, R))

    each(R, lambda d: y_copy(r, d).start(), 1)

    def m_copy(d):
        s = lax.rem(l + d, L)
        return remote(tiles.at[s, pl.ds(meta_at, metas)], mrecv.at[l], m_send.at[d], m_recv.at[l], s, r)

    each(L, lambda d: m_copy(d).start(), 1)
    mrecv[l] = tiles[l, pl.ds(meta_at, metas), :]

    each(R, lambda d: y_copy(lax.rem(r + d, R), d).wait_recv(), 1)

    w_own = w[pl.ds(pl.multiple_of(r * fs, fs), fs), :]
    for t in range(nt):
        whole = jnp.concatenate([yt[q, pl.ds(t * fs, fs), :] for q in range(R)], axis=0)
        pre = dot(wt[...], whole, NN) + biasb[...]
        sig = 0.5 + 0.5 * jnp.tanh(0.5 * pre)
        act_t[t] = (pre * sig).astype(BF)
        g = (cot_t[t].astype(F32) * sig * (1.0 + pre * (1.0 - sig))).astype(BF)
        grad[t] = g
        hid[pl.ds(t * fs, fs), :] = dot(w_own, g, NN)

    def q_copy(d):
        s = lax.rem(l + d, L)
        return remote(psend.at[s], precv.at[l], q_send.at[d], q_recv.at[l], s, r)

    def products(s, out, at):
        meta = tiles[s, pl.ds(meta_at, metas), :].astype(F32)
        blocks = [hid[pl.ds(t * fs, fs), :] for t in range(nt)]
        for k in range(slots):
            base = 2 * nt * k
            picked = sum(
                meta[base + t:base + t + 1, :] * blocks[t] for t in range(nt)
            ).astype(BF)
            out[at, pl.ds(k * fs, fs), :] = dot(
                picked, tiles[s, pl.ds(k * tile, tile), :], NN).astype(BF)

    def send_products(ds):
        for d in ds:
            s = lax.rem(l + L - d, L)
            products(s, psend, s)
        for d in ds:
            q_copy(L - d).start()

    groups(L, 4, send_products, 1)

    rp = f_in // L
    pad = wfin.shape[1] // 2
    gw = jnp.zeros((f_in, hidden), F32)
    gb = jnp.zeros((metas, hidden), F32)
    ones = jnp.ones((metas, tile), BF)
    for t in range(nt):
        whole = jnp.concatenate([yt[q, pl.ds(t * fs, fs), :] for q in range(R)], axis=0)
        gw = gw + dot(whole, grad[t], NT)
        gb = gb + dot(ones, grad[t], NT)

    def rows_of(value):
        if rp < pad:
            value = jnp.concatenate([value, jnp.zeros((pad - rp, tile), F32)], axis=0)
        return value.astype(BF)

    edge = lax.broadcasted_iota(jnp.int32, (metas, tile), 0)
    gb_rows = jnp.where(edge == 0, gb[:, :tile], jnp.where(edge == 1, gb[:, tile:], 0.0)).astype(BF)
    for p in range(L):
        for h in range(2):
            wsend[p, pl.ds(h * pad, pad), :] = rows_of(
                gw[p * rp:(p + 1) * rp, h * tile:(h + 1) * tile])
        wsend[p, pl.ds(2 * pad, metas), :] = gb_rows

    def w_copy(d):
        s = lax.rem(l + d, L)
        return remote(wsend.at[s], wrecv.at[l], w_send.at[d], w_recv.at[l], s, r)

    each(L, lambda d: w_copy(L - d).start(), 1)
    products(l, precv, l)
    wrecv[l] = wsend[l]

    for t in range(nt):
        act_o[pl.ds(t * tile, tile), :] = jnp.transpose(
            act_t[t].astype(F32), (1, 0)).astype(BF)

    def add_products(ids):
        sums = [hid[pl.ds(c * fs, fs), :] for c in range(nt)]
        for p in ids:
            meta = mrecv[p].astype(F32)
            for k in range(slots):
                part = precv[p, pl.ds(k * fs, fs), :].astype(F32)
                for c in range(nt):
                    at = 2 * nt * k + nt + c
                    sums[c] = sums[c] + meta[at:at + 1, :] * part
        for c in range(nt):
            hid[pl.ds(c * fs, fs), :] = sums[c]

    each(L, lambda d: remote(
        mrecv.at[lax.rem(l + d, L)], mrecv.at[lax.rem(l + d, L)], m_send.at[d],
        m_recv.at[lax.rem(l + d, L)], l, r).wait_recv(), 1)
    add_products([l])

    def take_products(ds):
        ids = [lax.rem(l + d, L) for d in ds]
        for d, p in zip(ds, ids):
            remote(precv.at[p], precv.at[p], q_send.at[d], q_recv.at[p], p, r).wait_recv()
        add_products(ids)

    groups(L, 2, take_products, 1)

    gft[r] = hid[...].astype(BF)

    def g_copy(q, d):
        return remote(gft.at[q], gft.at[q], g_send.at[d], g_recv.at[q], l, lax.rem(r + d, R))

    each(R, lambda d: g_copy(r, d).start(), 1)

    def w_wait(d):
        p = lax.rem(l + d, L)
        remote(wrecv.at[p], wrecv.at[p], w_send.at[d], w_recv.at[p], p, r).wait_recv()

    each(L, w_wait, 1)
    total = wrecv[0].astype(F32)
    for p in range(1, L):
        total = total + wrecv[p].astype(F32)
    total = total * grad_scale
    wfin[l] = total[:2 * pad].astype(BF)
    for h in range(2):
        gb_o[:, pl.ds(h * tile, tile)] = total[2 * pad + h:2 * pad + h + 1]

    def f_copy(p, d):
        return remote(wfin.at[p], wfin.at[p], f_send.at[d], f_recv.at[p], lax.rem(l + d, L), r)

    each(L, lambda d: f_copy(l, d).start(), 1)

    each(R, lambda d: g_copy(lax.rem(r + d, R), d).wait_recv(), 1)
    for t in range(nt):
        whole = jnp.concatenate([gft[q, pl.ds(t * fs, fs), :] for q in range(R)], axis=0)
        gf_o[pl.ds(t * tile, tile), :] = jnp.transpose(whole.astype(F32), (1, 0)).astype(BF)

    each(L, lambda d: f_copy(lax.rem(l + d, L), d).wait_recv(), 1)
    for p in range(L):
        for h in range(2):
            gw_o[pl.ds(p * rp, rp), pl.ds(h * tile, tile)] = (
                wfin[p, pl.ds(h * pad, pad), :].astype(F32)[:rp])

    each(R // 2, lambda d: t_direct(d).wait_send(), 1)
    each(R // 2, lambda d: t_forward(d).wait_send())
    each(L // 2, lambda d: x_direct(L // 2 - d).wait_send(), 1)
    each(L // 2, lambda d: x_forward(d).wait_send())

    def layer_sent(d):
        m_copy(d).wait_send()
        q_copy(d).wait_send()
        w_copy(d).wait_send()
        f_copy(l, d).wait_send()

    def rep_sent(d):
        y_copy(r, d).wait_send()
        g_copy(r, d).wait_send()

    each(L, layer_sent, 1)
    each(R, rep_sent, 1)


def write_kernel(*refs):
    n = (len(refs) - 1) // 2
    copies = [pltpu.make_async_copy(refs[i], refs[n + i], refs[-1].at[i]) for i in range(n)]
    for copy in copies:
        copy.start()
    for copy in copies:
        copy.wait()


def write_out(*arrays):
    n = len(arrays)
    return pl.pallas_call(
        write_kernel,
        out_shape=tuple(jax.ShapeDtypeStruct(a.shape, a.dtype) for a in arrays),
        in_specs=[pl.BlockSpec(memory_space=pltpu.VMEM)] * n,
        out_specs=(pl.BlockSpec(memory_space=pltpu.HBM),) * n,
        scratch_shapes=[pltpu.SemaphoreType.DMA((n,))],
        name="write_out",
    )(*[pltpu.with_memory_space_constraint(a, pltpu.VMEM) for a in arrays])


def local(features, weight, out_bias, tile_values, tile_rows, tile_cols, tile_counts, cotangent):
    L, R = lax.axis_size("layer"), lax.axis_size("rep")
    rows_dev, hidden = cotangent.shape
    f_in = features.shape[1]
    _, sections, slots, tile, _ = tile_values.shape
    nt = rows_dev // tile
    fs = f_in // R
    metas = slots * 2 * nt
    pad = -(-(f_in // L) // 16) * 16
    vmem = pl.BlockSpec(memory_space=pltpu.VMEM)
    hbm = pl.BlockSpec(memory_space=pltpu.HBM)
    sem = pltpu.SemaphoreType.DMA
    grad_scale = 1.0 / math.sqrt(rows_dev * L)
    act, gf, gw, gb = pl.pallas_call(
        functools.partial(kernel, L, R, grad_scale),
        out_shape=(
            jax.ShapeDtypeStruct((rows_dev, hidden), BF),
            jax.ShapeDtypeStruct((rows_dev, f_in), BF),
            jax.ShapeDtypeStruct((f_in, hidden), F32),
            jax.ShapeDtypeStruct((1, hidden), F32),
        ),
        in_specs=[hbm] * 8,
        out_specs=(vmem, vmem, vmem, vmem),
        scratch_shapes=[
            pltpu.VMEM(features.shape, BF),
            pltpu.VMEM(weight.shape, BF),
            pltpu.VMEM((1, hidden), F32),
            pltpu.SMEM(tile_rows.shape, jnp.int32),
            pltpu.SMEM(tile_rows.shape, jnp.int32),
            pltpu.SMEM(tile_rows.shape, jnp.int32),
            pltpu.VMEM(cotangent.shape, BF),
            sem((8,)),
            pltpu.VMEM((L, slots * tile + metas, tile), BF),
            pltpu.VMEM((L, nt * fs, tile), BF),
            pltpu.VMEM((R, nt * fs, tile), BF),
            pltpu.VMEM((hidden, f_in), BF),
            pltpu.VMEM((hidden, tile), F32),
            pltpu.VMEM((nt, hidden, tile), BF),
            pltpu.VMEM((nt, hidden, tile), BF),
            pltpu.VMEM((nt, hidden, tile), BF),
            pltpu.VMEM((nt * fs, tile), F32),
            pltpu.VMEM((L, slots * fs, tile), BF),
            pltpu.VMEM((L, slots * fs, tile), BF),
            pltpu.VMEM((L, metas, tile), BF),
            pltpu.VMEM((L, 2 * pad + metas, tile), BF),
            pltpu.VMEM((L, 2 * pad + metas, tile), BF),
            pltpu.VMEM((L, 2 * pad, tile), BF),
            pltpu.VMEM((R, nt * fs, tile), BF),
            sem((R,)), sem((R,)), sem((R,)),
            sem((L,)), sem((L,)), sem((L,)),
            sem((R,)), sem((R,)),
            sem((L,)), sem((L,)),
            sem((L,)), sem((L,)),
            sem((L,)), sem((L,)),
            sem((L,)), sem((L,)),
            sem((R,)), sem((R,)),
        ],
        compiler_params=pltpu.CompilerParams(
            collective_id=0, has_side_effects=True, vmem_limit_bytes=32 * 1024 * 1024
        ),
        name="graph_layer",
    )(*[pltpu.with_memory_space_constraint(x, pltpu.HBM) for x in (
        features, weight, out_bias.reshape(1, hidden),
        tile_values.reshape(sections, slots * tile, tile), tile_rows, tile_cols,
        tile_counts, cotangent)])
    return write_out(act, gf, gw, gb.reshape(hidden))


def solution(mesh):
    in_specs = (
        P("layer", None),
        P(),
        P(),
        P("layer", "rep", None, None, None),
        P("layer", "rep", None),
        P("layer", "rep", None),
        P("layer", "rep", None),
        P("layer", None),
    )
    out_specs = (P("layer", None), P("layer", None), P(), P())
    return jax.shard_map(local, mesh=mesh, in_specs=in_specs, out_specs=out_specs, check_vma=False)
```

```python
import functools
import math

import jax
import jax.numpy as jnp
from jax import lax
from jax.experimental import pallas as pl
from jax.experimental.pallas import tpu as pltpu
from jax.sharding import PartitionSpec as P

BF = jnp.bfloat16
F32 = jnp.float32
NT = (((1,), (1,)), ((), ()))
NN = (((1,), (0,)), ((), ()))
MESH = pl.DeviceIdType.MESH


def dot(a, b, dims):
    return lax.dot_general(a, b, dims, preferred_element_type=F32)


def kernel(
    L, R, grad_scale,
    feat_h, w_h, bias_h, tv_h, rows_h, cols_h, counts_h, cot_h,
    act_o, gf_o, gw_o, gb_o,
    feat, w, bias, rows, cols, counts, cot, in_sem,
    tiles, xt, yt, wt, biasb, cot_t, act_t, grad, hid, psend, precv, mrecv, wsend, wrecv, wfin, gft,
    t_send, t_recv, x_send, x_recv, y_send, y_recv, m_send, m_recv,
    q_send, q_recv, w_send, w_recv, f_send, e_send, f_recv, g_send, g_recv, a_send, a_recv, go, ready,
):
    l = lax.axis_index("layer")
    r = lax.axis_index("rep")
    H = R // 2
    h = r // 2
    works = lax.rem(r, 2) == 1
    twin = r + 1 - 2 * lax.rem(r, 2)
    tile = tiles.shape[2]
    sections = counts.shape[1]
    slots = counts.shape[2]
    f_in, hidden = w.shape
    fs = f_in // H
    nt = feat.shape[0] // tile
    meta_at = slots * tile
    metas = tiles.shape[1] - meta_at
    rp = f_in // L
    pad = wsend.shape[1] // 2

    def remote(src, dst, ssem, rsem, to_l, to_r):
        return pltpu.make_async_remote_copy(
            src_ref=src, dst_ref=dst, send_sem=ssem, recv_sem=rsem,
            device_id={"layer": to_l, "rep": to_r}, device_id_type=MESH,
        )

    def signal(sem, to_l, to_r):
        pl.semaphore_signal(sem, inc=1, device_id={"layer": to_l, "rep": to_r}, device_id_type=MESH)

    def each(n, fn, start=0):
        lax.fori_loop(start, n, lambda i, c: (fn(i), c)[1], 0)

    def groups(n, size, fn, start=0):
        if n <= 8:
            for i in range(start, n, size):
                fn(list(range(i, min(i + size, n))))
        else:
            each(n, lambda i: fn([i]), start)

    barrier = pltpu.get_barrier_semaphore()
    meta_loads = [
        pltpu.make_async_copy(src, dst, in_sem.at[i])
        for i, (src, dst) in enumerate((
            (counts_h, counts), (rows_h, rows), (cols_h, cols),
            (tv_h, tiles.at[pl.ds(r * sections, sections), pl.ds(0, meta_at)])))
    ]
    work_loads = [
        pltpu.make_async_copy(src, dst, in_sem.at[4 + i])
        for i, (src, dst) in enumerate(((feat_h, feat), (w_h, w), (bias_h, bias), (cot_h, cot)))
    ]
    for load in meta_loads[:3]:
        load.start()

    @pl.when(works)
    def _():
        work_loads[0].start()

    meta_loads[3].start()

    @pl.when(works)
    def _():
        for load in work_loads[1:]:
            load.start()
        each(L, lambda d: signal(barrier, lax.rem(l + d, L), r), 1)
        each(H, lambda d: signal(barrier, l, lax.rem(r + 2 * d, R)), 1)
        each(H, lambda d: signal(barrier, l, lax.rem(twin + 2 * d, R)))

    @pl.when(jnp.logical_not(works))
    def _():
        each(H, lambda d: signal(barrier, l, lax.rem(twin + 2 * d, R)))

    for load in meta_loads[:3]:
        load.wait()
    lanes = lax.broadcasted_iota(jnp.int32, (metas, tile), 1)
    row_ids = lax.broadcasted_iota(jnp.int32, (metas, tile), 0)
    for j in range(sections):
        meta = jnp.zeros((metas, tile), F32)
        for k in range(slots):
            base = 2 * nt * k
            meta = meta + jnp.where(row_ids == base + rows[0, j, k], 1.0, 0.0)
            live = jnp.where(lanes < counts[0, j, k], 1.0, 0.0)
            meta = meta + jnp.where(row_ids == base + nt + cols[0, j, k], live, 0.0)
        tiles[r * sections + j, pl.ds(meta_at, metas), :] = meta.astype(BF)

    def t_copy(d, j, to_r):
        s = r * sections + j
        return remote(tiles.at[s], tiles.at[s], t_send.at[d * sections + j], t_recv.at[s], l, to_r)

    def t_arrival(q, j):
        s = lax.rem(q, R) * sections + j
        return remote(tiles.at[s], tiles.at[s], t_send.at[0], t_recv.at[s], l, r)

    def g_copy(d, to_r):
        return remote(gft.at[h], gft.at[h], g_send.at[d], g_recv.at[h], l, to_r)

    def g_arrival(q):
        return remote(gft.at[q], gft.at[q], g_send.at[0], g_recv.at[q], l, r)

    def f_arrival(p):
        return remote(wfin.at[p], wfin.at[p], f_send.at[0], f_recv.at[p], l, r)

    act_copy = remote(act_o, act_o, a_send, a_recv, l, twin)

    def put_gf():
        for t in range(nt):
            whole = jnp.concatenate([gft[q, pl.ds(t * fs, fs), :] for q in range(H)], axis=0)
            gf_o[pl.ds(t * tile, tile), :] = jnp.transpose(whole.astype(F32), (1, 0)).astype(BF)

    def put_gw():
        total = jnp.zeros((metas, tile), F32)
        for p in range(L):
            total = total + wfin[p, pl.ds(2 * pad, metas), :].astype(F32)
            for i in range(2):
                gw_o[pl.ds(p * rp, rp), pl.ds(i * tile, tile)] = (
                    wfin[p, pl.ds(i * pad, pad), :].astype(F32)[:rp])
        total = total * grad_scale
        for i in range(2):
            gb_o[:, pl.ds(i * tile, tile)] = total[i:i + 1]

    @pl.when(jnp.logical_not(works))
    def _():
        meta_loads[3].wait()
        pl.semaphore_wait(barrier, H)

        def send(d):
            each(sections, lambda j: t_copy(d, j, lax.rem(twin + 2 * d, R)).start())

        each(H, lambda d: send(H - 1 - d))
        pl.semaphore_wait(go, 1)
        each(L, lambda d: signal(ready, lax.rem(l + d, L), twin))
        each(H, lambda d: each(sections, lambda j: t_copy(d, j, lax.rem(twin + 2 * d, R)).wait_send()))
        act_copy.wait_recv()
        each(H, lambda q: g_arrival(q).wait_recv())
        put_gf()
        each(L, lambda p: f_arrival(p).wait_recv())
        put_gw()

    @pl.when(works)
    def _():
        work_loads[0].wait()
        pick = (lax.broadcasted_iota(jnp.int32, (fs, f_in), 1)
                == h * fs + lax.broadcasted_iota(jnp.int32, (fs, f_in), 0))
        own = dot(jnp.where(pick, 1.0, 0.0).astype(BF), feat[...], NT).astype(BF)
        for t in range(nt):
            xt[l, pl.ds(t * fs, fs), :] = own[:, t * tile:(t + 1) * tile]
        meta_loads[3].wait()

        pl.semaphore_wait(barrier, L - 1 + H - 1 + H)

        def x_copy(d):
            return remote(xt.at[l], xt.at[l], x_send.at[d], x_recv.at[l], lax.rem(l + d, L), r)

        def x_arrival(d):
            p = lax.rem(l + d, L)
            return remote(xt.at[p], xt.at[p], x_send.at[d], x_recv.at[p], p, r)

        each(L, lambda d: x_copy(d).start(), 1)
        each(H, lambda d: each(sections, lambda j: t_copy(d, j, lax.rem(r + 2 * d, R)).start()), 1)

        for load in work_loads[1:]:
            load.wait()
        wt[...] = jnp.transpose(w[...].astype(F32), (1, 0)).astype(BF)
        biasb[...] = jnp.transpose(jnp.broadcast_to(bias[...], (tile, hidden)), (1, 0))
        for t in range(nt):
            part = cot[pl.ds(t * tile, tile), :].astype(F32)
            cot_t[t] = jnp.transpose(part, (1, 0)).astype(BF)
        hid[...] = xt[l].astype(F32)
        each(H, lambda d: each(sections, lambda j: t_arrival(twin + 2 * d, j).wait_recv()))
        each(H, lambda d: each(sections, lambda j: t_arrival(r + 2 * d, j).wait_recv()), 1)

        def gather_sections(ids):
            sums = [hid[pl.ds(t * fs, fs), :] for t in range(nt)]
            for s in ids:
                meta = tiles[s, pl.ds(meta_at, metas), :].astype(F32)
                blocks = [xt[s, pl.ds(c * fs, fs), :].astype(F32) for c in range(nt)]
                for k in range(slots):
                    base = 2 * nt * k
                    picked = sum(
                        meta[base + nt + c:base + nt + c + 1, :] * blocks[c] for c in range(nt)
                    ).astype(BF)
                    product = dot(picked, tiles[s, pl.ds(k * tile, tile), :], NT)
                    for t in range(nt):
                        sums[t] = sums[t] + meta[base + t:base + t + 1, :] * product
            for t in range(nt):
                hid[pl.ds(t * fs, fs), :] = sums[t]

        def take_sections(ds):
            for d in ds:
                if not isinstance(d, int) or d:
                    x_arrival(d).wait_recv()
            gather_sections([lax.rem(l + d, L) for d in ds])

        gather_sections([l])
        groups(L, 2, take_sections, 1)

        yt[h] = hid[...].astype(BF)

        def y_copy(d):
            return remote(yt.at[h], yt.at[h], y_send.at[d], y_recv.at[h], l, lax.rem(r + 2 * d, R))

        def y_arrival(d):
            q = lax.rem(h + d, H)
            return remote(yt.at[q], yt.at[q], y_send.at[d], y_recv.at[q], l, r)

        each(H, lambda d: y_copy(d).start(), 1)
        signal(go, l, twin)

        def m_copy(d):
            s = lax.rem(l + d, L)
            return remote(tiles.at[s, pl.ds(meta_at, metas)], mrecv.at[l], m_send.at[d], m_recv.at[l], s, r)

        def m_arrival(d):
            p = lax.rem(l + d, L)
            return remote(mrecv.at[p], mrecv.at[p], m_send.at[d], m_recv.at[p], p, r)

        each(L, lambda d: m_copy(d).start(), 1)
        mrecv[l] = tiles[l, pl.ds(meta_at, metas), :]
        each(L, lambda d: x_copy(d).wait_send(), 1)
        each(H, lambda d: each(sections, lambda j: t_copy(d, j, lax.rem(r + 2 * d, R)).wait_send()), 1)
        each(H, lambda d: y_arrival(d).wait_recv(), 1)

        w_own = w[pl.ds(pl.multiple_of(h * fs, fs), fs), :]
        for t in range(nt):
            whole = jnp.concatenate([yt[q, pl.ds(t * fs, fs), :] for q in range(H)], axis=0)
            pre = dot(wt[...], whole, NN) + biasb[...]
            sig = 0.5 + 0.5 * jnp.tanh(0.5 * pre)
            act_t[t] = (pre * sig).astype(BF)
            g = (cot_t[t].astype(F32) * sig * (1.0 + pre * (1.0 - sig))).astype(BF)
            grad[t] = g
            hid[pl.ds(t * fs, fs), :] = dot(w_own, g, NN)

        def q_copy(d):
            s = lax.rem(l + d, L)
            return remote(psend.at[s], precv.at[l], q_send.at[d], q_recv.at[l], s, r)

        def q_arrival(d):
            p = lax.rem(l + d, L)
            return remote(precv.at[p], precv.at[p], q_send.at[d], q_recv.at[p], p, r)

        def products(s, out, at):
            meta = tiles[s, pl.ds(meta_at, metas), :].astype(F32)
            blocks = [hid[pl.ds(t * fs, fs), :] for t in range(nt)]
            for k in range(slots):
                base = 2 * nt * k
                picked = sum(
                    meta[base + t:base + t + 1, :] * blocks[t] for t in range(nt)
                ).astype(BF)
                out[at, pl.ds(k * fs, fs), :] = dot(
                    picked, tiles[s, pl.ds(k * tile, tile), :], NN).astype(BF)

        def send_products(ds):
            for d in ds:
                s = lax.rem(l + L - d, L)
                products(s, psend, s)
            for d in ds:
                q_copy(L - d).start()

        def w_copy(d):
            s = lax.rem(l + d, L)
            return remote(wsend.at[s], wrecv.at[l], w_send.at[d], w_recv.at[l], s, r)

        def w_arrival(d):
            p = lax.rem(l + d, L)
            return remote(wrecv.at[p], wrecv.at[p], w_send.at[d], w_recv.at[p], p, r)

        def rows_of(value):
            if rp < pad:
                value = jnp.concatenate([value, jnp.zeros((pad - rp, tile), F32)], axis=0)
            return value.astype(BF)

        groups(L, 4, send_products, 1)

        gw = jnp.zeros((f_in, hidden), F32)
        gb = jnp.zeros((metas, hidden), F32)
        ones = jnp.ones((metas, tile), BF)
        for t in range(nt):
            whole = jnp.concatenate([yt[q, pl.ds(t * fs, fs), :] for q in range(H)], axis=0)
            gw = gw + dot(whole, grad[t], NT)
            gb = gb + dot(ones, grad[t], NT)
        for p in range(L):
            for i in range(2):
                wsend[p, pl.ds(i * pad, pad), :] = rows_of(
                    gw[p * rp:(p + 1) * rp, i * tile:(i + 1) * tile])
        each(L, lambda d: w_copy(L - d).start(), 1)
        edge = lax.broadcasted_iota(jnp.int32, (metas, tile), 0)
        gb_rows = jnp.where(edge == 0, gb[:, :tile], jnp.where(edge == 1, gb[:, tile:], 0.0))
        wfin[l, pl.ds(2 * pad, metas), :] = gb_rows.astype(BF)
        wrecv[l] = wsend[l]
        products(l, precv, l)

        for t in range(nt):
            act_o[pl.ds(t * tile, tile), :] = jnp.transpose(
                act_t[t].astype(F32), (1, 0)).astype(BF)
        act_copy.start()

        each(L, lambda d: m_arrival(d).wait_recv(), 1)
        each(L, lambda d: m_copy(d).wait_send(), 1)
        each(H, lambda d: y_copy(d).wait_send(), 1)
        pl.semaphore_wait(ready, L)

        def add_products(ids):
            sums = [hid[pl.ds(c * fs, fs), :] for c in range(nt)]
            for p in ids:
                meta = mrecv[p].astype(F32)
                for k in range(slots):
                    part = precv[p, pl.ds(k * fs, fs), :].astype(F32)
                    for c in range(nt):
                        at = 2 * nt * k + nt + c
                        sums[c] = sums[c] + meta[at:at + 1, :] * part
            for c in range(nt):
                hid[pl.ds(c * fs, fs), :] = sums[c]

        def take_products(ds):
            for d in ds:
                q_arrival(d).wait_recv()
            add_products([lax.rem(l + d, L) for d in ds])

        add_products([l])
        groups(L, 2, take_products, 1)
        gft[h] = hid[...].astype(BF)
        each(H, lambda d: g_copy(d, lax.rem(twin + 2 * (H - 1 - d), R)).start())
        each(H, lambda d: g_copy(H - 1 + d, lax.rem(r + 2 * d, R)).start(), 1)

        each(L, lambda d: w_arrival(d).wait_recv(), 1)
        total = wrecv[0].astype(F32)
        for p in range(1, L):
            total = total + wrecv[p].astype(F32)
        wfin[l, pl.ds(0, 2 * pad), :] = (total * grad_scale).astype(BF)

        def f_copy(d):
            return remote(wfin.at[l], wfin.at[l], f_send.at[d], f_recv.at[l], lax.rem(l + d, L), r)

        def e_copy(d):
            return remote(wfin.at[l], wfin.at[l], e_send.at[d], f_recv.at[l], lax.rem(l + d, L), twin)

        each(L, lambda d: e_copy(d).start())
        each(L, lambda d: f_copy(d).start(), 1)
        act_copy.wait_send()
        each(L, lambda d: q_copy(d).wait_send(), 1)
        each(L, lambda d: w_copy(d).wait_send(), 1)

        each(H, lambda d: g_arrival(lax.rem(h + d, H)).wait_recv(), 1)
        put_gf()
        each(L, lambda d: f_arrival(lax.rem(l + d, L)).wait_recv(), 1)
        put_gw()

        each(2 * H - 1, lambda d: g_copy(d, twin).wait_send())
        each(L, lambda d: e_copy(d).wait_send())
        each(L, lambda d: f_copy(d).wait_send(), 1)


def write_kernel(*refs):
    n = (len(refs) - 1) // 2
    copies = [pltpu.make_async_copy(refs[i], refs[n + i], refs[-1].at[i]) for i in range(n)]
    for copy in copies:
        copy.start()
    for copy in copies:
        copy.wait()


def write_out(*arrays):
    n = len(arrays)
    return pl.pallas_call(
        write_kernel,
        out_shape=tuple(jax.ShapeDtypeStruct(a.shape, a.dtype) for a in arrays),
        in_specs=[pl.BlockSpec(memory_space=pltpu.VMEM)] * n,
        out_specs=(pl.BlockSpec(memory_space=pltpu.HBM),) * n,
        scratch_shapes=[pltpu.SemaphoreType.DMA((n,))],
        name="write_out",
    )(*[pltpu.with_memory_space_constraint(a, pltpu.VMEM) for a in arrays])


def local(features, weight, out_bias, tile_values, tile_rows, tile_cols, tile_counts, cotangent):
    L, R = lax.axis_size("layer"), lax.axis_size("rep")
    H = R // 2
    rows_dev, hidden = cotangent.shape
    f_in = features.shape[1]
    _, sections, slots, tile, _ = tile_values.shape
    nt = rows_dev // tile
    fs = f_in // H
    metas = slots * 2 * nt
    pad = -(-(f_in // L) // 16) * 16
    vmem = pl.BlockSpec(memory_space=pltpu.VMEM)
    hbm = pl.BlockSpec(memory_space=pltpu.HBM)
    sem = pltpu.SemaphoreType.DMA
    regular = pltpu.SemaphoreType.REGULAR
    grad_scale = 1.0 / math.sqrt(rows_dev * L)
    act, gf, gw, gb = pl.pallas_call(
        functools.partial(kernel, L, R, grad_scale),
        out_shape=(
            jax.ShapeDtypeStruct((rows_dev, hidden), BF),
            jax.ShapeDtypeStruct((rows_dev, f_in), BF),
            jax.ShapeDtypeStruct((f_in, hidden), F32),
            jax.ShapeDtypeStruct((1, hidden), F32),
        ),
        in_specs=[hbm] * 8,
        out_specs=(vmem, vmem, vmem, vmem),
        scratch_shapes=[
            pltpu.VMEM(features.shape, BF),
            pltpu.VMEM(weight.shape, BF),
            pltpu.VMEM((1, hidden), F32),
            pltpu.SMEM(tile_rows.shape, jnp.int32),
            pltpu.SMEM(tile_rows.shape, jnp.int32),
            pltpu.SMEM(tile_rows.shape, jnp.int32),
            pltpu.VMEM(cotangent.shape, BF),
            sem((8,)),
            pltpu.VMEM((L, slots * tile + metas, tile), BF),
            pltpu.VMEM((L, nt * fs, tile), BF),
            pltpu.VMEM((H, nt * fs, tile), BF),
            pltpu.VMEM((hidden, f_in), BF),
            pltpu.VMEM((hidden, tile), F32),
            pltpu.VMEM((nt, hidden, tile), BF),
            pltpu.VMEM((nt, hidden, tile), BF),
            pltpu.VMEM((nt, hidden, tile), BF),
            pltpu.VMEM((nt * fs, tile), F32),
            pltpu.VMEM((L, slots * fs, tile), BF),
            pltpu.VMEM((L, slots * fs, tile), BF),
            pltpu.VMEM((L, metas, tile), BF),
            pltpu.VMEM((L, 2 * pad, tile), BF),
            pltpu.VMEM((L, 2 * pad, tile), BF),
            pltpu.VMEM((L, 2 * pad + metas, tile), BF),
            pltpu.VMEM((H, nt * fs, tile), BF),
            sem((H * sections,)), sem((L,)),
            sem((L,)), sem((L,)),
            sem((H,)), sem((H,)),
            sem((L,)), sem((L,)),
            sem((L,)), sem((L,)),
            sem((L,)), sem((L,)),
            sem((L,)), sem((L,)), sem((L,)),
            sem((R,)), sem((H,)),
            sem, sem,
            regular, regular,
        ],
        compiler_params=pltpu.CompilerParams(
            collective_id=0, has_side_effects=True, vmem_limit_bytes=32 * 1024 * 1024
        ),
        name="graph_layer",
    )(*[pltpu.with_memory_space_constraint(x, pltpu.HBM) for x in (
        features, weight, out_bias.reshape(1, hidden),
        tile_values.reshape(sections, slots * tile, tile), tile_rows, tile_cols,
        tile_counts, cotangent)])
    return write_out(act, gf, gw, gb.reshape(hidden))


def solution(mesh):
    in_specs = (
        P("layer", None),
        P(),
        P(),
        P("layer", "rep", None, None, None),
        P("layer", "rep", None),
        P("layer", "rep", None),
        P("layer", "rep", None),
        P("layer", None),
    )
    out_specs = (P("layer", None), P("layer", None), P(), P())
    return jax.shard_map(local, mesh=mesh, in_specs=in_specs, out_specs=out_specs, check_vma=False)
```

```python
import functools
import math

import jax
import jax.numpy as jnp
from jax import lax
from jax.experimental import pallas as pl
from jax.experimental.pallas import tpu as pltpu
from jax.sharding import PartitionSpec as P

BF = jnp.bfloat16
F32 = jnp.float32
NT = (((1,), (1,)), ((), ()))
NN = (((1,), (0,)), ((), ()))
MESH = pl.DeviceIdType.MESH


def dot(a, b, dims):
    return lax.dot_general(a, b, dims, preferred_element_type=F32)


def flip(value):
    size = value.shape[1]
    eye = (lax.broadcasted_iota(jnp.int32, (size, size), 0)
           == lax.broadcasted_iota(jnp.int32, (size, size), 1))
    return dot(jnp.where(eye, 1.0, 0.0).astype(BF), value, NT).astype(BF)


def kernel(
    L, R, grad_scale,
    feat_h, w_h, bias_h, tv_h, rows_h, cols_h, counts_h, cot_h,
    act_o, gf_o, gw_o, gb_o,
    feat, w, bias, rows, cols, counts, cot, in_sem,
    tiles, xt, yt, wt, biasb, cot_t, act_t, grad, hid, psend, precv, mrecv, wsend, wrecv, wfin, gft,
    t_send, t_recv, x_send, x_recv, y_send, y_recv, m_send, m_recv,
    q_send, q_recv, w_send, w_recv, f_send, e_send, f_recv, g_send, g_recv, a_send, a_recv, go, ready,
):
    l = lax.axis_index("layer")
    r = lax.axis_index("rep")
    H = R // 2
    h = r // 2
    works = lax.rem(r, 2) == 1
    twin = r + 1 - 2 * lax.rem(r, 2)
    tile = tiles.shape[2]
    sections = counts.shape[1]
    slots = counts.shape[2]
    f_in, hidden = w.shape
    fs = f_in // H
    nt = feat.shape[0] // tile
    meta_at = slots * tile
    metas = tiles.shape[1] - meta_at
    rp = f_in // L
    pad = wsend.shape[1] // 2

    def remote(src, dst, ssem, rsem, to_l, to_r):
        return pltpu.make_async_remote_copy(
            src_ref=src, dst_ref=dst, send_sem=ssem, recv_sem=rsem,
            device_id={"layer": to_l, "rep": to_r}, device_id_type=MESH,
        )

    def signal(sem, to_l, to_r):
        pl.semaphore_signal(sem, inc=1, device_id={"layer": to_l, "rep": to_r}, device_id_type=MESH)

    def each(n, fn, start=0):
        lax.fori_loop(start, n, lambda i, c: (fn(i), c)[1], 0)

    def groups(n, size, fn, start=0):
        if n <= 8:
            for i in range(start, n, size):
                fn(list(range(i, min(i + size, n))))
        else:
            each(n, lambda i: fn([i]), start)

    def other(i):
        return i + jnp.where(i >= l, 1, 0)

    def nearest(i):
        return other(jnp.where(2 * l < L, i, L - 2 - i))

    barrier = pltpu.get_barrier_semaphore()
    meta_loads = [
        pltpu.make_async_copy(src, dst, in_sem.at[i])
        for i, (src, dst) in enumerate((
            (counts_h, counts), (rows_h, rows), (cols_h, cols),
            (tv_h, tiles.at[pl.ds(r * sections, sections), pl.ds(0, meta_at)])))
    ]
    work_loads = [
        pltpu.make_async_copy(src, dst, in_sem.at[4 + i])
        for i, (src, dst) in enumerate(((feat_h, feat), (w_h, w), (bias_h, bias), (cot_h, cot)))
    ]
    for load in meta_loads[:3]:
        load.start()

    @pl.when(works)
    def _():
        work_loads[0].start()

    meta_loads[3].start()

    @pl.when(works)
    def _():
        for load in work_loads[1:]:
            load.start()
        each(L, lambda d: signal(barrier, lax.rem(l + d, L), r), 1)
        each(H, lambda d: signal(barrier, l, lax.rem(r + 2 * d, R)), 1)
        each(H, lambda d: signal(barrier, l, lax.rem(twin + 2 * d, R)))

    @pl.when(jnp.logical_not(works))
    def _():
        each(H, lambda d: signal(barrier, l, lax.rem(twin + 2 * d, R)))

    for load in meta_loads[:3]:
        load.wait()
    lanes = lax.broadcasted_iota(jnp.int32, (metas, tile), 1)
    row_ids = lax.broadcasted_iota(jnp.int32, (metas, tile), 0)
    for j in range(sections):
        meta = jnp.zeros((metas, tile), F32)
        for k in range(slots):
            base = 2 * nt * k
            meta = meta + jnp.where(row_ids == base + rows[0, j, k], 1.0, 0.0)
            live = jnp.where(lanes < counts[0, j, k], 1.0, 0.0)
            meta = meta + jnp.where(row_ids == base + nt + cols[0, j, k], live, 0.0)
        tiles[r * sections + j, pl.ds(meta_at, metas), :] = meta.astype(BF)

    def t_copy(d, j, to_r):
        s = r * sections + j
        return remote(tiles.at[s], tiles.at[s], t_send.at[d * sections + j], t_recv.at[s], l, to_r)

    def t_arrival(q, j):
        s = lax.rem(q, R) * sections + j
        return remote(tiles.at[s], tiles.at[s], t_send.at[0], t_recv.at[s], l, r)

    def g_copy(d, to_r):
        return remote(gft.at[h], gft.at[h], g_send.at[d], g_recv.at[h], l, to_r)

    def g_arrival(q):
        return remote(gft.at[q], gft.at[q], g_send.at[0], g_recv.at[q], l, r)

    f_some = remote(wfin.at[pl.ds(0, L - 1)], wfin.at[pl.ds(0, L - 1)], f_send, f_recv, l, r)
    f_all = remote(wfin, wfin, e_send, f_recv, l, r)

    act_copy = remote(act_o, act_o, a_send, a_recv, l, twin)

    def put_gf():
        for t in range(nt):
            whole = jnp.concatenate([gft[q, pl.ds(t * fs, fs), :] for q in range(H)], axis=0)
            gf_o[pl.ds(t * tile, tile), :] = flip(whole)

    def put_gw():
        total = jnp.zeros((metas, tile), F32)
        for p in range(L):
            total = total + wfin[p, pl.ds(2 * pad, metas), :].astype(F32)
            for i in range(2):
                gw_o[pl.ds(p * rp, rp), pl.ds(i * tile, tile)] = (
                    wfin[p, pl.ds(i * pad, pad), :].astype(F32)[:rp])
        total = total * grad_scale
        for i in range(2):
            gb_o[:, pl.ds(i * tile, tile)] = total[i:i + 1]

    @pl.when(jnp.logical_not(works))
    def _():
        meta_loads[3].wait()
        pl.semaphore_wait(barrier, H)

        def send(d):
            each(sections, lambda j: t_copy(d, j, lax.rem(twin + 2 * d, R)).start())

        each(H, lambda d: send(H - 1 - d))
        pl.semaphore_wait(go, 1)
        each(L, lambda d: signal(ready, lax.rem(l + d, L), twin))
        each(H, lambda d: each(sections, lambda j: t_copy(d, j, lax.rem(twin + 2 * d, R)).wait_send()))
        act_copy.wait_recv()
        each(H, lambda q: g_arrival(q).wait_recv())
        put_gf()
        f_all.wait_recv()
        put_gw()

    @pl.when(works)
    def _():
        work_loads[0].wait()
        pick = (lax.broadcasted_iota(jnp.int32, (fs, f_in), 1)
                == h * fs + lax.broadcasted_iota(jnp.int32, (fs, f_in), 0))
        own = dot(jnp.where(pick, 1.0, 0.0).astype(BF), feat[...], NT).astype(BF)
        for t in range(nt):
            xt[l, pl.ds(t * fs, fs), :] = own[:, t * tile:(t + 1) * tile]
        meta_loads[3].wait()

        pl.semaphore_wait(barrier, L - 1 + H - 1 + H)

        def x_copy(i):
            return remote(xt.at[l], xt.at[l], x_send.at[i], x_recv.at[l], other(i), r)

        def x_arrival(i):
            p = nearest(i)
            return remote(xt.at[p], xt.at[p], x_send.at[i], x_recv.at[p], p, r)

        each(L - 1, lambda i: x_copy(L - 2 - i).start())
        each(H, lambda d: each(sections, lambda j: t_copy(d, j, lax.rem(r + 2 * d, R)).start()), 1)

        for load in work_loads[1:]:
            load.wait()
        wt[...] = flip(w[...])
        biasb[...] = jnp.transpose(jnp.broadcast_to(bias[...], (tile, hidden)), (1, 0))
        for t in range(nt):
            cot_t[t] = flip(cot[pl.ds(t * tile, tile), :])
        hid[...] = xt[l].astype(F32)
        each(H, lambda d: each(sections, lambda j: t_arrival(twin + 2 * d, j).wait_recv()))
        each(H, lambda d: each(sections, lambda j: t_arrival(r + 2 * d, j).wait_recv()), 1)

        def gather_sections(ids):
            sums = [hid[pl.ds(t * fs, fs), :] for t in range(nt)]
            for s in ids:
                meta = tiles[s, pl.ds(meta_at, metas), :].astype(F32)
                blocks = [xt[s, pl.ds(c * fs, fs), :].astype(F32) for c in range(nt)]
                for k in range(slots):
                    base = 2 * nt * k
                    picked = sum(
                        meta[base + nt + c:base + nt + c + 1, :] * blocks[c] for c in range(nt)
                    ).astype(BF)
                    product = dot(picked, tiles[s, pl.ds(k * tile, tile), :], NT)
                    for t in range(nt):
                        sums[t] = sums[t] + meta[base + t:base + t + 1, :] * product
            for t in range(nt):
                hid[pl.ds(t * fs, fs), :] = sums[t]

        def take_sections(ds):
            for d in ds:
                x_arrival(d).wait_recv()
            gather_sections([nearest(d) for d in ds])

        gather_sections([l])
        groups(L - 1, 2, take_sections)

        yt[h] = hid[...].astype(BF)

        def y_copy(d):
            return remote(yt.at[h], yt.at[h], y_send.at[d], y_recv.at[h], l, lax.rem(r + 2 * d, R))

        def y_arrival(d):
            q = lax.rem(h + d, H)
            return remote(yt.at[q], yt.at[q], y_send.at[d], y_recv.at[q], l, r)

        each(H, lambda d: y_copy(d).start(), 1)
        signal(go, l, twin)

        def m_copy(d):
            s = lax.rem(l + d, L)
            return remote(tiles.at[s, pl.ds(meta_at, metas)], mrecv.at[l], m_send.at[d], m_recv.at[l], s, r)

        def m_arrival(d):
            p = lax.rem(l + d, L)
            return remote(mrecv.at[p], mrecv.at[p], m_send.at[d], m_recv.at[p], p, r)

        each(L, lambda d: m_copy(d).start(), 1)
        mrecv[l] = tiles[l, pl.ds(meta_at, metas), :]
        each(L - 1, lambda i: x_copy(i).wait_send())
        each(H, lambda d: each(sections, lambda j: t_copy(d, j, lax.rem(r + 2 * d, R)).wait_send()), 1)
        each(H, lambda d: y_arrival(d).wait_recv(), 1)

        w_own = w[pl.ds(pl.multiple_of(h * fs, fs), fs), :]
        for t in range(nt):
            whole = jnp.concatenate([yt[q, pl.ds(t * fs, fs), :] for q in range(H)], axis=0)
            pre = dot(wt[...], whole, NN) + biasb[...]
            sig = 0.5 + 0.5 * jnp.tanh(0.5 * pre)
            act_t[t] = (pre * sig).astype(BF)
            g = (cot_t[t].astype(F32) * sig * (1.0 + pre * (1.0 - sig))).astype(BF)
            grad[t] = g
            hid[pl.ds(t * fs, fs), :] = dot(w_own, g, NN)

        def q_copy(i):
            s = other(i)
            return remote(psend.at[s], precv.at[l], q_send.at[i], q_recv.at[l], s, r)

        def q_arrival(i):
            p = nearest(i)
            return remote(precv.at[p], precv.at[p], q_send.at[i], q_recv.at[p], p, r)

        def products(s, out, at):
            meta = tiles[s, pl.ds(meta_at, metas), :].astype(F32)
            blocks = [hid[pl.ds(t * fs, fs), :] for t in range(nt)]
            for k in range(slots):
                base = 2 * nt * k
                picked = sum(
                    meta[base + t:base + t + 1, :] * blocks[t] for t in range(nt)
                ).astype(BF)
                out[at, pl.ds(k * fs, fs), :] = dot(
                    picked, tiles[s, pl.ds(k * tile, tile), :], NN).astype(BF)

        def send_products(ds):
            for d in ds:
                products(other(d), psend, other(d))
            for d in ds:
                q_copy(d).start()

        def w_copy(i):
            s = other(i)
            return remote(wsend.at[s], wrecv.at[l], w_send, w_recv, s, r)

        w_all = remote(wrecv.at[pl.ds(0, L - 1)], wrecv.at[pl.ds(0, L - 1)], w_send, w_recv, l, r)

        def rows_of(value):
            if rp < pad:
                value = jnp.concatenate([value, jnp.zeros((pad - rp, tile), F32)], axis=0)
            return value.astype(BF)

        gw = jnp.zeros((f_in, hidden), F32)
        gb = jnp.zeros((metas, hidden), F32)
        ones = jnp.ones((metas, tile), BF)
        for t in range(nt):
            whole = jnp.concatenate([yt[q, pl.ds(t * fs, fs), :] for q in range(H)], axis=0)
            gw = gw + dot(whole, grad[t], NT)
            gb = gb + dot(ones, grad[t], NT)
        for p in range(L):
            for i in range(2):
                wsend[p, pl.ds(i * pad, pad), :] = rows_of(
                    gw[p * rp:(p + 1) * rp, i * tile:(i + 1) * tile])
        each(L - 1, lambda i: w_copy(i).start())
        groups(L - 1, 4, send_products)
        edge = lax.broadcasted_iota(jnp.int32, (metas, tile), 0)
        gb_rows = jnp.where(edge == 0, gb[:, :tile], jnp.where(edge == 1, gb[:, tile:], 0.0))
        wfin[l, pl.ds(2 * pad, metas), :] = gb_rows.astype(BF)
        wrecv[l] = wsend[l]
        products(l, precv, l)

        for t in range(nt):
            act_o[pl.ds(t * tile, tile), :] = flip(act_t[t])
        act_copy.start()

        each(L, lambda d: m_arrival(d).wait_recv(), 1)
        each(L, lambda d: m_copy(d).wait_send(), 1)
        each(H, lambda d: y_copy(d).wait_send(), 1)
        pl.semaphore_wait(ready, L)

        w_all.wait_recv()
        total = wrecv[0].astype(F32)
        for p in range(1, L):
            total = total + wrecv[p].astype(F32)
        wfin[l, pl.ds(0, 2 * pad), :] = (total * grad_scale).astype(BF)

        def f_copy(d):
            return remote(wfin.at[l], wfin.at[l], f_send, f_recv, other(d), r)

        def e_copy(d):
            return remote(wfin.at[l], wfin.at[l], e_send, f_recv, d, twin)

        each(L, lambda d: e_copy(d).start())
        each(L - 1, lambda d: f_copy(d).start())

        def add_products(ids):
            sums = [hid[pl.ds(c * fs, fs), :] for c in range(nt)]
            for p in ids:
                meta = mrecv[p].astype(F32)
                for k in range(slots):
                    part = precv[p, pl.ds(k * fs, fs), :].astype(F32)
                    for c in range(nt):
                        at = 2 * nt * k + nt + c
                        sums[c] = sums[c] + meta[at:at + 1, :] * part
            for c in range(nt):
                hid[pl.ds(c * fs, fs), :] = sums[c]

        def take_products(ds):
            for d in ds:
                q_arrival(d).wait_recv()
            add_products([nearest(d) for d in ds])

        add_products([l])
        groups(L - 1, 2, take_products)
        gft[h] = hid[...].astype(BF)
        each(H, lambda d: g_copy(d, lax.rem(twin + 2 * (H - 1 - d), R)).start())
        each(H, lambda d: g_copy(H - 1 + d, lax.rem(r + 2 * d, R)).start(), 1)

        act_copy.wait_send()
        each(L - 1, lambda i: q_copy(i).wait_send())
        w_all.wait_send()

        each(H, lambda d: g_arrival(lax.rem(h + d, H)).wait_recv(), 1)
        put_gf()
        f_some.wait_recv()
        put_gw()

        each(2 * H - 1, lambda d: g_copy(d, twin).wait_send())
        f_all.wait_send()
        f_some.wait_send()


def write_kernel(*refs):
    n = (len(refs) - 1) // 2
    copies = [pltpu.make_async_copy(refs[i], refs[n + i], refs[-1].at[i]) for i in range(n)]
    for copy in copies:
        copy.start()
    for copy in copies:
        copy.wait()


def write_out(*arrays):
    n = len(arrays)
    return pl.pallas_call(
        write_kernel,
        out_shape=tuple(jax.ShapeDtypeStruct(a.shape, a.dtype) for a in arrays),
        in_specs=[pl.BlockSpec(memory_space=pltpu.VMEM)] * n,
        out_specs=(pl.BlockSpec(memory_space=pltpu.HBM),) * n,
        scratch_shapes=[pltpu.SemaphoreType.DMA((n,))],
        name="write_out",
    )(*[pltpu.with_memory_space_constraint(a, pltpu.VMEM) for a in arrays])


def local(features, weight, out_bias, tile_values, tile_rows, tile_cols, tile_counts, cotangent):
    L, R = lax.axis_size("layer"), lax.axis_size("rep")
    H = R // 2
    rows_dev, hidden = cotangent.shape
    f_in = features.shape[1]
    _, sections, slots, tile, _ = tile_values.shape
    nt = rows_dev // tile
    fs = f_in // H
    metas = slots * 2 * nt
    pad = -(-(f_in // L) // 16) * 16
    vmem = pl.BlockSpec(memory_space=pltpu.VMEM)
    hbm = pl.BlockSpec(memory_space=pltpu.HBM)
    sem = pltpu.SemaphoreType.DMA
    regular = pltpu.SemaphoreType.REGULAR
    grad_scale = 1.0 / math.sqrt(rows_dev * L)
    act, gf, gw, gb = pl.pallas_call(
        functools.partial(kernel, L, R, grad_scale),
        out_shape=(
            jax.ShapeDtypeStruct((rows_dev, hidden), BF),
            jax.ShapeDtypeStruct((rows_dev, f_in), BF),
            jax.ShapeDtypeStruct((f_in, hidden), F32),
            jax.ShapeDtypeStruct((1, hidden), F32),
        ),
        in_specs=[hbm] * 8,
        out_specs=(vmem, vmem, vmem, vmem),
        scratch_shapes=[
            pltpu.VMEM(features.shape, BF),
            pltpu.VMEM(weight.shape, BF),
            pltpu.VMEM((1, hidden), F32),
            pltpu.SMEM(tile_rows.shape, jnp.int32),
            pltpu.SMEM(tile_rows.shape, jnp.int32),
            pltpu.SMEM(tile_rows.shape, jnp.int32),
            pltpu.VMEM(cotangent.shape, BF),
            sem((8,)),
            pltpu.VMEM((L, slots * tile + metas, tile), BF),
            pltpu.VMEM((L, nt * fs, tile), BF),
            pltpu.VMEM((H, nt * fs, tile), BF),
            pltpu.VMEM((hidden, f_in), BF),
            pltpu.VMEM((hidden, tile), F32),
            pltpu.VMEM((nt, hidden, tile), BF),
            pltpu.VMEM((nt, hidden, tile), BF),
            pltpu.VMEM((nt, hidden, tile), BF),
            pltpu.VMEM((nt * fs, tile), F32),
            pltpu.VMEM((L, slots * fs, tile), BF),
            pltpu.VMEM((L, slots * fs, tile), BF),
            pltpu.VMEM((L, metas, tile), BF),
            pltpu.VMEM((L, 2 * pad, tile), BF),
            pltpu.VMEM((L, 2 * pad, tile), BF),
            pltpu.VMEM((L, 2 * pad + metas, tile), BF),
            pltpu.VMEM((H, nt * fs, tile), BF),
            sem((H * sections,)), sem((L,)),
            sem((L,)), sem((L,)),
            sem((H,)), sem((H,)),
            sem((L,)), sem((L,)),
            sem((L,)), sem((L,)),
            sem, sem,
            sem, sem, sem,
            sem((R,)), sem((H,)),
            sem, sem,
            regular, regular,
        ],
        compiler_params=pltpu.CompilerParams(
            collective_id=0, has_side_effects=True, vmem_limit_bytes=32 * 1024 * 1024
        ),
        name="graph_layer",
    )(*[pltpu.with_memory_space_constraint(x, pltpu.HBM) for x in (
        features, weight, out_bias.reshape(1, hidden),
        tile_values.reshape(sections, slots * tile, tile), tile_rows, tile_cols,
        tile_counts, cotangent)])
    return write_out(act, gf, gw, gb.reshape(hidden))


def solution(mesh):
    in_specs = (
        P("layer", None),
        P(),
        P(),
        P("layer", "rep", None, None, None),
        P("layer", "rep", None),
        P("layer", "rep", None),
        P("layer", "rep", None),
        P("layer", None),
    )
    out_specs = (P("layer", None), P("layer", None), P(), P())
    return jax.shard_map(local, mesh=mesh, in_specs=in_specs, out_specs=out_specs, check_vma=False)
```

```python
import functools
import math

import jax
import jax.numpy as jnp
from jax import lax
from jax.experimental import pallas as pl
from jax.experimental.pallas import tpu as pltpu
from jax.sharding import PartitionSpec as P

BF = jnp.bfloat16
F32 = jnp.float32
NT = (((1,), (1,)), ((), ()))
NN = (((1,), (0,)), ((), ()))
MESH = pl.DeviceIdType.MESH


def dot(a, b, dims):
    return lax.dot_general(a, b, dims, preferred_element_type=F32)


def flip(value):
    size = value.shape[1]
    eye = (lax.broadcasted_iota(jnp.int32, (size, size), 0)
           == lax.broadcasted_iota(jnp.int32, (size, size), 1))
    return dot(jnp.where(eye, 1.0, 0.0).astype(BF), value, NT).astype(BF)


def kernel(
    L, R, grad_scale,
    feat_h, w_h, bias_h, tv_h, rows_h, cols_h, counts_h, cot_h,
    act_o, gf_o, gw_o, gb_o,
    feat, w, bias, rows, cols, counts, cot, in_sem,
    tiles, xt, yt, wt, biasb, cot_t, act_t, grad, hid, psend, precv, mrecv, wsend, wrecv, wfin, gft,
    t_send, t_recv, x_send, x_fwd, x_recv, y_send, y_recv, m_send, m_recv,
    q_send, q_recv, w_send, w_recv, f_send, e_send, f_recv, g_send, g_recv, a_send, a_recv, go, ready,
):
    l = lax.axis_index("layer")
    r = lax.axis_index("rep")
    H = R // 2
    h = r // 2
    Z = L // 2
    z = l // 2
    y = lax.rem(l, 2)
    twin_l = l + 1 - 2 * y
    works = lax.rem(r, 2) == 1
    twin = r + 1 - 2 * lax.rem(r, 2)
    tile = tiles.shape[2]
    sections = counts.shape[1]
    slots = counts.shape[2]
    f_in, hidden = w.shape
    fs = f_in // H
    nt = feat.shape[0] // tile
    meta_at = slots * tile
    metas = tiles.shape[1] - meta_at
    rp = f_in // L
    pad = wsend.shape[1] // 2

    def remote(src, dst, ssem, rsem, to_l, to_r):
        return pltpu.make_async_remote_copy(
            src_ref=src, dst_ref=dst, send_sem=ssem, recv_sem=rsem,
            device_id={"layer": to_l, "rep": to_r}, device_id_type=MESH,
        )

    def signal(sem, to_l, to_r):
        pl.semaphore_signal(sem, inc=1, device_id={"layer": to_l, "rep": to_r}, device_id_type=MESH)

    def each(n, fn, start=0):
        lax.fori_loop(start, n, lambda i, c: (fn(i), c)[1], 0)

    def groups(n, size, fn, start=0):
        if n <= 8:
            for i in range(start, n, size):
                fn(list(range(i, min(i + size, n))))
        else:
            each(n, lambda i: fn([i]), start)

    def other(i):
        return i + jnp.where(i >= l, 1, 0)

    def nearest(i):
        return other(jnp.where(2 * l < L, i, L - 2 - i))

    barrier = pltpu.get_barrier_semaphore()
    meta_loads = [
        pltpu.make_async_copy(src, dst, in_sem.at[i])
        for i, (src, dst) in enumerate((
            (counts_h, counts), (rows_h, rows), (cols_h, cols),
            (tv_h, tiles.at[pl.ds(r * sections, sections), pl.ds(0, meta_at)])))
    ]
    work_loads = [
        pltpu.make_async_copy(src, dst, in_sem.at[4 + i])
        for i, (src, dst) in enumerate(((feat_h, feat), (w_h, w), (bias_h, bias), (cot_h, cot)))
    ]
    for load in meta_loads[:3]:
        load.start()

    @pl.when(works)
    def _():
        work_loads[0].start()

    meta_loads[3].start()

    @pl.when(works)
    def _():
        for load in work_loads[1:]:
            load.start()
        each(L, lambda d: signal(barrier, lax.rem(l + d, L), r), 1)
        each(H, lambda d: signal(barrier, l, lax.rem(r + 2 * d, R)), 1)
        each(H, lambda d: signal(barrier, l, lax.rem(twin + 2 * d, R)))

    @pl.when(jnp.logical_not(works))
    def _():
        each(H, lambda d: signal(barrier, l, lax.rem(twin + 2 * d, R)))

    for load in meta_loads[:3]:
        load.wait()
    lanes = lax.broadcasted_iota(jnp.int32, (metas, tile), 1)
    row_ids = lax.broadcasted_iota(jnp.int32, (metas, tile), 0)
    for j in range(sections):
        meta = jnp.zeros((metas, tile), F32)
        for k in range(slots):
            base = 2 * nt * k
            meta = meta + jnp.where(row_ids == base + rows[0, j, k], 1.0, 0.0)
            live = jnp.where(lanes < counts[0, j, k], 1.0, 0.0)
            meta = meta + jnp.where(row_ids == base + nt + cols[0, j, k], live, 0.0)
        tiles[r * sections + j, pl.ds(meta_at, metas), :] = meta.astype(BF)

    def t_copy(d, j, to_r):
        s = r * sections + j
        return remote(tiles.at[s], tiles.at[s], t_send.at[d * sections + j], t_recv.at[s], l, to_r)

    def t_arrival(q, j):
        s = lax.rem(q, R) * sections + j
        return remote(tiles.at[s], tiles.at[s], t_send.at[0], t_recv.at[s], l, r)

    def g_copy(d, to_r):
        return remote(gft.at[h], gft.at[h], g_send.at[d], g_recv.at[h], l, to_r)

    def g_arrival(q):
        return remote(gft.at[q], gft.at[q], g_send.at[0], g_recv.at[q], l, r)

    f_some = remote(wfin.at[pl.ds(0, L - 1)], wfin.at[pl.ds(0, L - 1)], f_send, f_recv, l, r)
    f_all = remote(wfin, wfin, e_send, f_recv, l, r)

    act_copy = remote(act_o, act_o, a_send, a_recv, l, twin)

    def put_gf():
        for t in range(nt):
            whole = jnp.concatenate([gft[q, pl.ds(t * fs, fs), :] for q in range(H)], axis=0)
            gf_o[pl.ds(t * tile, tile), :] = flip(whole)

    def put_gw():
        total = jnp.zeros((metas, tile), F32)
        for p in range(L):
            total = total + wfin[p, pl.ds(2 * pad, metas), :].astype(F32)
            for i in range(2):
                gw_o[pl.ds(p * rp, rp), pl.ds(i * tile, tile)] = (
                    wfin[p, pl.ds(i * pad, pad), :].astype(F32)[:rp])
        total = total * grad_scale
        for i in range(2):
            gb_o[:, pl.ds(i * tile, tile)] = total[i:i + 1]

    @pl.when(jnp.logical_not(works))
    def _():
        meta_loads[3].wait()
        pl.semaphore_wait(barrier, H)

        def send(d):
            each(sections, lambda j: t_copy(d, j, lax.rem(twin + 2 * d, R)).start())

        each(H, lambda d: send(H - 1 - d))
        pl.semaphore_wait(go, 1)
        each(L, lambda d: signal(ready, lax.rem(l + d, L), twin))
        each(H, lambda d: each(sections, lambda j: t_copy(d, j, lax.rem(twin + 2 * d, R)).wait_send()))
        act_copy.wait_recv()
        each(H, lambda q: g_arrival(q).wait_recv())
        put_gf()
        f_all.wait_recv()
        put_gw()

    @pl.when(works)
    def _():
        work_loads[0].wait()
        pick = (lax.broadcasted_iota(jnp.int32, (fs, f_in), 1)
                == h * fs + lax.broadcasted_iota(jnp.int32, (fs, f_in), 0))
        own = dot(jnp.where(pick, 1.0, 0.0).astype(BF), feat[...], NT).astype(BF)
        for t in range(nt):
            xt[l, pl.ds(t * fs, fs), :] = own[:, t * tile:(t + 1) * tile]
        meta_loads[3].wait()

        pl.semaphore_wait(barrier, L - 1 + H - 1 + H)

        def pair(i):
            i = jnp.where(2 * z < Z, i, Z - 2 - i)
            return i + jnp.where(i >= z, 1, 0)

        def near(i):
            return (pair(i) - z <= 2) & (z - pair(i) <= 2)

        def x_copy(i):
            return remote(xt.at[l], xt.at[l], x_send.at[2 * i], x_recv.at[l], 2 * pair(i) + y, r)

        def x_cross(i):
            return remote(xt.at[l], xt.at[l], x_send.at[2 * i + 1], x_recv.at[l], 2 * pair(i) + 1 - y, r)

        def x_relay(p, i):
            return remote(xt.at[p], xt.at[p], x_fwd.at[i], x_recv.at[p], twin_l, r)

        def x_start(i):
            @pl.when(jnp.logical_not(near(i)))
            def _():
                x_cross(i).start()

            x_copy(i).start()

        def x_pass(i):
            p = 2 * pair(i) + y
            x_relay(p, i).wait_recv()

            @pl.when(near(i))
            def _():
                x_relay(p, i).start()

        def x_sent(i):
            x_copy(i).wait_send()

            @pl.when(near(i))
            def _():
                x_relay(2 * pair(i) + y, i).wait_send()

            @pl.when(jnp.logical_not(near(i)))
            def _():
                x_cross(i).wait_send()

        x_relay(l, Z - 1).start()
        each(Z - 1, lambda i: x_start(i))
        each(H, lambda d: each(sections, lambda j: t_copy(d, j, lax.rem(r + 2 * d, R)).start()), 1)

        for load in work_loads[1:]:
            load.wait()
        wt[...] = flip(w[...])
        biasb[...] = jnp.transpose(jnp.broadcast_to(bias[...], (tile, hidden)), (1, 0))
        for t in range(nt):
            cot_t[t] = flip(cot[pl.ds(t * tile, tile), :])
        hid[...] = xt[l].astype(F32)
        each(Z - 1, x_pass)
        each(H, lambda d: each(sections, lambda j: t_arrival(twin + 2 * d, j).wait_recv()))
        each(H, lambda d: each(sections, lambda j: t_arrival(r + 2 * d, j).wait_recv()), 1)

        def gather_sections(ids):
            sums = [hid[pl.ds(t * fs, fs), :] for t in range(nt)]
            for s in ids:
                meta = tiles[s, pl.ds(meta_at, metas), :].astype(F32)
                blocks = [xt[s, pl.ds(c * fs, fs), :].astype(F32) for c in range(nt)]
                for k in range(slots):
                    base = 2 * nt * k
                    picked = sum(
                        meta[base + nt + c:base + nt + c + 1, :] * blocks[c] for c in range(nt)
                    ).astype(BF)
                    product = dot(picked, tiles[s, pl.ds(k * tile, tile), :], NT)
                    for t in range(nt):
                        sums[t] = sums[t] + meta[base + t:base + t + 1, :] * product
            for t in range(nt):
                hid[pl.ds(t * fs, fs), :] = sums[t]

        groups(Z, 4, lambda ds: gather_sections([2 * d + y for d in ds]))

        def take_sections(ds):
            ids = [2 * d + 1 - y for d in ds]
            for p in ids:
                x_relay(p, 0).wait_recv()
            gather_sections(ids)

        groups(Z, 2, take_sections)

        yt[h] = hid[...].astype(BF)

        def y_copy(d):
            return remote(yt.at[h], yt.at[h], y_send.at[d], y_recv.at[h], l, lax.rem(r + 2 * d, R))

        def y_arrival(d):
            q = lax.rem(h + d, H)
            return remote(yt.at[q], yt.at[q], y_send.at[d], y_recv.at[q], l, r)

        each(H, lambda d: y_copy(d).start(), 1)
        signal(go, l, twin)

        def m_copy(d):
            s = lax.rem(l + d, L)
            return remote(tiles.at[s, pl.ds(meta_at, metas)], mrecv.at[l], m_send.at[d], m_recv.at[l], s, r)

        def m_arrival(d):
            p = lax.rem(l + d, L)
            return remote(mrecv.at[p], mrecv.at[p], m_send.at[d], m_recv.at[p], p, r)

        each(L, lambda d: m_copy(d).start(), 1)
        mrecv[l] = tiles[l, pl.ds(meta_at, metas), :]
        each(Z - 1, x_sent)
        x_relay(l, Z - 1).wait_send()
        each(H, lambda d: each(sections, lambda j: t_copy(d, j, lax.rem(r + 2 * d, R)).wait_send()), 1)
        each(H, lambda d: y_arrival(d).wait_recv(), 1)

        w_own = w[pl.ds(pl.multiple_of(h * fs, fs), fs), :]
        for t in range(nt):
            whole = jnp.concatenate([yt[q, pl.ds(t * fs, fs), :] for q in range(H)], axis=0)
            pre = dot(wt[...], whole, NN) + biasb[...]
            sig = 0.5 + 0.5 * jnp.tanh(0.5 * pre)
            act_t[t] = (pre * sig).astype(BF)
            g = (cot_t[t].astype(F32) * sig * (1.0 + pre * (1.0 - sig))).astype(BF)
            grad[t] = g
            hid[pl.ds(t * fs, fs), :] = dot(w_own, g, NN)

        def q_copy(i):
            s = other(i)
            return remote(psend.at[s], precv.at[l], q_send.at[i], q_recv.at[l], s, r)

        def q_arrival(i):
            p = nearest(i)
            return remote(precv.at[p], precv.at[p], q_send.at[i], q_recv.at[p], p, r)

        def products(s, out, at):
            meta = tiles[s, pl.ds(meta_at, metas), :].astype(F32)
            blocks = [hid[pl.ds(t * fs, fs), :] for t in range(nt)]
            for k in range(slots):
                base = 2 * nt * k
                picked = sum(
                    meta[base + t:base + t + 1, :] * blocks[t] for t in range(nt)
                ).astype(BF)
                out[at, pl.ds(k * fs, fs), :] = dot(
                    picked, tiles[s, pl.ds(k * tile, tile), :], NN).astype(BF)

        def send_products(ds):
            for d in ds:
                products(other(d), psend, other(d))
            for d in ds:
                q_copy(d).start()

        def w_copy(i):
            s = other(i)
            return remote(wsend.at[s], wrecv.at[l], w_send, w_recv, s, r)

        w_all = remote(wrecv.at[pl.ds(0, L - 1)], wrecv.at[pl.ds(0, L - 1)], w_send, w_recv, l, r)

        def rows_of(value):
            if rp < pad:
                value = jnp.concatenate([value, jnp.zeros((pad - rp, tile), F32)], axis=0)
            return value.astype(BF)

        gw = jnp.zeros((f_in, hidden), F32)
        for t in range(nt):
            whole = jnp.concatenate([yt[q, pl.ds(t * fs, fs), :] for q in range(H)], axis=0)
            gw = gw + dot(whole, grad[t], NT)
        for p in range(L):
            for i in range(2):
                wsend[p, pl.ds(i * pad, pad), :] = rows_of(
                    gw[p * rp:(p + 1) * rp, i * tile:(i + 1) * tile])
        each(L - 1, lambda i: w_copy(L - 2 - i).start())
        groups(L - 1, 4, send_products)
        ones = jnp.ones((metas, tile), BF)
        gb = sum(dot(ones, grad[t], NT) for t in range(nt))
        edge = lax.broadcasted_iota(jnp.int32, (metas, tile), 0)
        gb_rows = jnp.where(edge == 0, gb[:, :tile], jnp.where(edge == 1, gb[:, tile:], 0.0))
        wfin[l, pl.ds(2 * pad, metas), :] = gb_rows.astype(BF)
        wrecv[l] = wsend[l]
        products(l, precv, l)

        for t in range(nt):
            act_o[pl.ds(t * tile, tile), :] = flip(act_t[t])
        act_copy.start()

        each(L, lambda d: m_arrival(d).wait_recv(), 1)
        each(L, lambda d: m_copy(d).wait_send(), 1)
        each(H, lambda d: y_copy(d).wait_send(), 1)
        pl.semaphore_wait(ready, L)

        w_all.wait_recv()
        total = wrecv[0].astype(F32)
        for p in range(1, L):
            total = total + wrecv[p].astype(F32)
        wfin[l, pl.ds(0, 2 * pad), :] = (total * grad_scale).astype(BF)

        def f_copy(d):
            return remote(wfin.at[l], wfin.at[l], f_send, f_recv, other(d), r)

        def e_copy(d):
            return remote(wfin.at[l], wfin.at[l], e_send, f_recv, d, twin)

        each(L, lambda d: e_copy(d).start())
        each(L - 1, lambda d: f_copy(d).start())

        def add_products(ids):
            sums = [hid[pl.ds(c * fs, fs), :] for c in range(nt)]
            for p in ids:
                meta = mrecv[p].astype(F32)
                for k in range(slots):
                    part = precv[p, pl.ds(k * fs, fs), :].astype(F32)
                    for c in range(nt):
                        at = 2 * nt * k + nt + c
                        sums[c] = sums[c] + meta[at:at + 1, :] * part
            for c in range(nt):
                hid[pl.ds(c * fs, fs), :] = sums[c]

        def take_products(ds):
            for d in ds:
                q_arrival(d).wait_recv()
            add_products([nearest(d) for d in ds])

        add_products([l])
        groups(L - 1, 2, take_products)
        gft[h] = hid[...].astype(BF)
        each(H, lambda d: g_copy(d, lax.rem(twin + 2 * (H - 1 - d), R)).start())
        each(H, lambda d: g_copy(H - 1 + d, lax.rem(r + 2 * d, R)).start(), 1)

        act_copy.wait_send()
        each(L - 1, lambda i: q_copy(i).wait_send())
        w_all.wait_send()

        each(H, lambda d: g_arrival(lax.rem(h + d, H)).wait_recv(), 1)
        put_gf()
        f_some.wait_recv()
        put_gw()

        each(2 * H - 1, lambda d: g_copy(d, twin).wait_send())
        f_all.wait_send()
        f_some.wait_send()


def write_kernel(*refs):
    n = (len(refs) - 1) // 2
    copies = [pltpu.make_async_copy(refs[i], refs[n + i], refs[-1].at[i]) for i in range(n)]
    for copy in copies:
        copy.start()
    for copy in copies:
        copy.wait()


def write_out(*arrays):
    n = len(arrays)
    return pl.pallas_call(
        write_kernel,
        out_shape=tuple(jax.ShapeDtypeStruct(a.shape, a.dtype) for a in arrays),
        in_specs=[pl.BlockSpec(memory_space=pltpu.VMEM)] * n,
        out_specs=(pl.BlockSpec(memory_space=pltpu.HBM),) * n,
        scratch_shapes=[pltpu.SemaphoreType.DMA((n,))],
        name="write_out",
    )(*[pltpu.with_memory_space_constraint(a, pltpu.VMEM) for a in arrays])


def local(features, weight, out_bias, tile_values, tile_rows, tile_cols, tile_counts, cotangent):
    L, R = lax.axis_size("layer"), lax.axis_size("rep")
    H = R // 2
    rows_dev, hidden = cotangent.shape
    f_in = features.shape[1]
    _, sections, slots, tile, _ = tile_values.shape
    nt = rows_dev // tile
    fs = f_in // H
    metas = slots * 2 * nt
    pad = -(-(f_in // L) // 16) * 16
    vmem = pl.BlockSpec(memory_space=pltpu.VMEM)
    hbm = pl.BlockSpec(memory_space=pltpu.HBM)
    sem = pltpu.SemaphoreType.DMA
    regular = pltpu.SemaphoreType.REGULAR
    grad_scale = 1.0 / math.sqrt(rows_dev * L)
    act, gf, gw, gb = pl.pallas_call(
        functools.partial(kernel, L, R, grad_scale),
        out_shape=(
            jax.ShapeDtypeStruct((rows_dev, hidden), BF),
            jax.ShapeDtypeStruct((rows_dev, f_in), BF),
            jax.ShapeDtypeStruct((f_in, hidden), F32),
            jax.ShapeDtypeStruct((1, hidden), F32),
        ),
        in_specs=[hbm] * 8,
        out_specs=(vmem, vmem, vmem, vmem),
        scratch_shapes=[
            pltpu.VMEM(features.shape, BF),
            pltpu.VMEM(weight.shape, BF),
            pltpu.VMEM((1, hidden), F32),
            pltpu.SMEM(tile_rows.shape, jnp.int32),
            pltpu.SMEM(tile_rows.shape, jnp.int32),
            pltpu.SMEM(tile_rows.shape, jnp.int32),
            pltpu.VMEM(cotangent.shape, BF),
            sem((8,)),
            pltpu.VMEM((L, slots * tile + metas, tile), BF),
            pltpu.VMEM((L, nt * fs, tile), BF),
            pltpu.VMEM((H, nt * fs, tile), BF),
            pltpu.VMEM((hidden, f_in), BF),
            pltpu.VMEM((hidden, tile), F32),
            pltpu.VMEM((nt, hidden, tile), BF),
            pltpu.VMEM((nt, hidden, tile), BF),
            pltpu.VMEM((nt, hidden, tile), BF),
            pltpu.VMEM((nt * fs, tile), F32),
            pltpu.VMEM((L, slots * fs, tile), BF),
            pltpu.VMEM((L, slots * fs, tile), BF),
            pltpu.VMEM((L, metas, tile), BF),
            pltpu.VMEM((L, 2 * pad, tile), BF),
            pltpu.VMEM((L, 2 * pad, tile), BF),
            pltpu.VMEM((L, 2 * pad + metas, tile), BF),
            pltpu.VMEM((H, nt * fs, tile), BF),
            sem((H * sections,)), sem((L,)),
            sem((L,)), sem((L,)), sem((L,)),
            sem((H,)), sem((H,)),
            sem((L,)), sem((L,)),
            sem((L,)), sem((L,)),
            sem, sem,
            sem, sem, sem,
            sem((R,)), sem((H,)),
            sem, sem,
            regular, regular,
        ],
        compiler_params=pltpu.CompilerParams(
            collective_id=0, has_side_effects=True, vmem_limit_bytes=32 * 1024 * 1024
        ),
        name="graph_layer",
    )(*[pltpu.with_memory_space_constraint(x, pltpu.HBM) for x in (
        features, weight, out_bias.reshape(1, hidden),
        tile_values.reshape(sections, slots * tile, tile), tile_rows, tile_cols,
        tile_counts, cotangent)])
    return write_out(act, gf, gw, gb.reshape(hidden))


def solution(mesh):
    in_specs = (
        P("layer", None),
        P(),
        P(),
        P("layer", "rep", None, None, None),
        P("layer", "rep", None),
        P("layer", "rep", None),
        P("layer", "rep", None),
        P("layer", None),
    )
    out_specs = (P("layer", None), P("layer", None), P(), P())
    return jax.shard_map(local, mesh=mesh, in_specs=in_specs, out_specs=out_specs, check_vma=False)
```

```python
import functools
import math

import jax
import jax.numpy as jnp
from jax import lax
from jax.experimental import pallas as pl
from jax.experimental.pallas import tpu as pltpu
from jax.sharding import PartitionSpec as P

BF = jnp.bfloat16
F32 = jnp.float32
NT = (((1,), (1,)), ((), ()))
NN = (((1,), (0,)), ((), ()))
MESH = pl.DeviceIdType.MESH


def dot(a, b, dims):
    return lax.dot_general(a, b, dims, preferred_element_type=F32)


def flip(value):
    size = value.shape[1]
    eye = (lax.broadcasted_iota(jnp.int32, (size, size), 0)
           == lax.broadcasted_iota(jnp.int32, (size, size), 1))
    return dot(jnp.where(eye, 1.0, 0.0).astype(BF), value, NT).astype(BF)


def kernel(
    L, R, grad_scale,
    feat_h, w_h, bias_h, tv_h, rows_h, cols_h, counts_h, cot_h,
    act_o, gf_o, gw_o, gb_o,
    feat, w, bias, rows, cols, counts, cot, in_sem,
    tiles, xt, yt, wt, biasb, cot_t, act_t, grad, hid, psend, precv, mrecv, wsend, wrecv, wfin, gft,
    t_send, t_recv, x_send, x_fwd, x_recv, y_send, y_recv, m_send, m_recv,
    q_send, q_recv, w_send, w_recv, f_send, e_send, f_recv, g_send, g_recv, a_send, a_recv, go, ready,
):
    l = lax.axis_index("layer")
    r = lax.axis_index("rep")
    H = R // 2
    h = r // 2
    Z = L // 2
    z = l // 2
    y = lax.rem(l, 2)
    twin_l = l + 1 - 2 * y
    works_r = 2 * h + 1
    works = lax.rem(r, 2) == 1
    twin = r + 1 - 2 * lax.rem(r, 2)
    tile = tiles.shape[2]
    sections = counts.shape[1]
    slots = counts.shape[2]
    f_in, hidden = w.shape
    fs = f_in // H
    nt = feat.shape[0] // tile
    meta_at = slots * tile
    metas = tiles.shape[1] - meta_at
    rp = f_in // L
    pad = wsend.shape[1] // 2

    def remote(src, dst, ssem, rsem, to_l, to_r):
        return pltpu.make_async_remote_copy(
            src_ref=src, dst_ref=dst, send_sem=ssem, recv_sem=rsem,
            device_id={"layer": to_l, "rep": to_r}, device_id_type=MESH,
        )

    def signal(sem, to_l, to_r):
        pl.semaphore_signal(sem, inc=1, device_id={"layer": to_l, "rep": to_r}, device_id_type=MESH)

    def each(n, fn, start=0):
        lax.fori_loop(start, n, lambda i, c: (fn(i), c)[1], 0)

    def groups(n, size, fn, start=0):
        if n <= 8:
            for i in range(start, n, size):
                fn(list(range(i, min(i + size, n))))
        else:
            each(n, lambda i: fn([i]), start)

    def other(i):
        return i + jnp.where(i >= l, 1, 0)

    def nearest(i):
        return other(jnp.where(2 * l < L, i, L - 2 - i))

    barrier = pltpu.get_barrier_semaphore()
    meta_loads = [
        pltpu.make_async_copy(src, dst, in_sem.at[i])
        for i, (src, dst) in enumerate((
            (counts_h, counts), (rows_h, rows), (cols_h, cols), (feat_h, feat),
            (tv_h, tiles.at[pl.ds(r * sections, sections), pl.ds(0, meta_at)])))
    ]
    work_loads = [
        pltpu.make_async_copy(src, dst, in_sem.at[5 + i])
        for i, (src, dst) in enumerate(((w_h, w), (bias_h, bias), (cot_h, cot)))
    ]
    meta_loads[3].start()

    @pl.when(works)
    def _():
        each(L, lambda d: signal(barrier, lax.rem(l + d, L), r), 1)
        each(L, lambda d: signal(barrier, lax.rem(l + d, L), twin), 1)
        each(H, lambda d: signal(barrier, l, lax.rem(r + 2 * d, R)), 1)

    each(H, lambda d: signal(barrier, l, lax.rem(twin + 2 * d, R)))
    for load in meta_loads[:3] + meta_loads[4:]:
        load.start()

    @pl.when(works)
    def _():
        for load in work_loads:
            load.start()

    for load in meta_loads[:3]:
        load.wait()
    lanes = lax.broadcasted_iota(jnp.int32, (metas, tile), 1)
    row_ids = lax.broadcasted_iota(jnp.int32, (metas, tile), 0)
    for j in range(sections):
        meta = jnp.zeros((metas, tile), F32)
        for k in range(slots):
            base = 2 * nt * k
            meta = meta + jnp.where(row_ids == base + rows[0, j, k], 1.0, 0.0)
            live = jnp.where(lanes < counts[0, j, k], 1.0, 0.0)
            meta = meta + jnp.where(row_ids == base + nt + cols[0, j, k], live, 0.0)
        tiles[r * sections + j, pl.ds(meta_at, metas), :] = meta.astype(BF)

    meta_loads[3].wait()
    pick = (lax.broadcasted_iota(jnp.int32, (fs, f_in), 1)
            == h * fs + lax.broadcasted_iota(jnp.int32, (fs, f_in), 0))
    own = dot(jnp.where(pick, 1.0, 0.0).astype(BF), feat[...], NT).astype(BF)
    for t in range(nt):
        xt[l, pl.ds(t * fs, fs), :] = own[:, t * tile:(t + 1) * tile]

    def pair(i):
        i = jnp.where(2 * z < Z, i, Z - 2 - i)
        return i + jnp.where(i >= z, 1, 0)

    def x_copy(i, p, to_r):
        return remote(xt.at[l], xt.at[l], x_send.at[i], x_recv.at[l], p, to_r)

    def x_same(i):
        return x_copy(2 * i, 2 * pair(i) + y, works_r)

    def x_cross(i):
        return x_copy(2 * i + 1, 2 * pair(i) + 1 - y, works_r)

    def within(i, reach):
        return (pair(i) - z <= reach) & (z - pair(i) <= reach)

    def x_pass(i):
        p = 2 * pair(i) + y
        return remote(xt.at[p], xt.at[p], x_fwd.at[i], x_recv.at[p], twin_l, r)

    def on_worker(do):
        def visit(i):
            @pl.when(within(i, 8))
            def _():
                do(x_same(i))

        each(Z - 1, visit)

    def on_other(do):
        do(x_twin())

        def visit(i):
            @pl.when(jnp.logical_not(within(i, 8)))
            def _():
                do(x_same(i))

            @pl.when(jnp.logical_not(within(i, 1)))
            def _():
                do(x_cross(i))

        each(Z - 1, visit)

    def x_twin():
        return x_copy(L - 1, twin_l, works_r)

    def x_arrival(p):
        return remote(xt.at[p], xt.at[p], x_send.at[0], x_recv.at[p], p, r)

    def t_copy(d, j, to_r):
        s = r * sections + j
        return remote(tiles.at[s], tiles.at[s], t_send.at[d * sections + j], t_recv.at[s], l, to_r)

    def t_arrival(q, j):
        s = lax.rem(q, R) * sections + j
        return remote(tiles.at[s], tiles.at[s], t_send.at[0], t_recv.at[s], l, r)

    def g_copy(d, to_r):
        return remote(gft.at[h], gft.at[h], g_send.at[d], g_recv.at[h], l, to_r)

    def g_arrival(q):
        return remote(gft.at[q], gft.at[q], g_send.at[0], g_recv.at[q], l, r)

    f_some = remote(wfin.at[pl.ds(0, L - 1)], wfin.at[pl.ds(0, L - 1)], f_send, f_recv, l, r)
    f_all = remote(wfin, wfin, e_send, f_recv, l, r)

    act_copy = remote(act_o, act_o, a_send, a_recv, l, twin)

    def put_gf():
        for t in range(nt):
            whole = jnp.concatenate([gft[q, pl.ds(t * fs, fs), :] for q in range(H)], axis=0)
            gf_o[pl.ds(t * tile, tile), :] = flip(whole)

    def put_gw():
        total = jnp.zeros((metas, tile), F32)
        for p in range(L):
            total = total + wfin[p, pl.ds(2 * pad, metas), :].astype(F32)
            for i in range(2):
                gw_o[pl.ds(p * rp, rp), pl.ds(i * tile, tile)] = (
                    wfin[p, pl.ds(i * pad, pad), :].astype(F32)[:rp])
        total = total * grad_scale
        for i in range(2):
            gb_o[:, pl.ds(i * tile, tile)] = total[i:i + 1]

    @pl.when(jnp.logical_not(works))
    def _():
        meta_loads[4].wait()
        pl.semaphore_wait(barrier, H + L - 1)

        def send(d):
            each(sections, lambda j: t_copy(d, j, lax.rem(twin + 2 * d, R)).start())

        on_other(lambda copy: copy.start())
        each(H, lambda d: send(H - 1 - d))
        pl.semaphore_wait(go, 1)
        each(L, lambda d: signal(ready, lax.rem(l + d, L), twin))
        each(H, lambda d: each(sections, lambda j: t_copy(d, j, lax.rem(twin + 2 * d, R)).wait_send()))
        on_other(lambda copy: copy.wait_send())
        act_copy.wait_recv()
        each(H, lambda q: g_arrival(q).wait_recv())
        put_gf()
        f_all.wait_recv()
        put_gw()

    @pl.when(works)
    def _():
        meta_loads[4].wait()

        pl.semaphore_wait(barrier, L - 1 + H - 1 + H)

        on_worker(lambda copy: copy.start())
        each(H, lambda d: each(sections, lambda j: t_copy(d, j, lax.rem(r + 2 * d, R)).start()), 1)

        for load in work_loads:
            load.wait()
        wt[...] = flip(w[...])
        biasb[...] = jnp.transpose(jnp.broadcast_to(bias[...], (tile, hidden)), (1, 0))
        for t in range(nt):
            cot_t[t] = flip(cot[pl.ds(t * tile, tile), :])
        hid[...] = xt[l].astype(F32)

        def x_take(i):
            x_pass(i).wait_recv()

            @pl.when(within(i, 1))
            def _():
                x_pass(i).start()

        each(Z - 1, x_take)
        each(H, lambda d: each(sections, lambda j: t_arrival(twin + 2 * d, j).wait_recv()))
        each(H, lambda d: each(sections, lambda j: t_arrival(r + 2 * d, j).wait_recv()), 1)

        def gather_sections(ids):
            sums = [hid[pl.ds(t * fs, fs), :] for t in range(nt)]
            for s in ids:
                meta = tiles[s, pl.ds(meta_at, metas), :].astype(F32)
                blocks = [xt[s, pl.ds(c * fs, fs), :].astype(F32) for c in range(nt)]
                for k in range(slots):
                    base = 2 * nt * k
                    picked = sum(
                        meta[base + nt + c:base + nt + c + 1, :] * blocks[c] for c in range(nt)
                    ).astype(BF)
                    product = dot(picked, tiles[s, pl.ds(k * tile, tile), :], NT)
                    for t in range(nt):
                        sums[t] = sums[t] + meta[base + t:base + t + 1, :] * product
            for t in range(nt):
                hid[pl.ds(t * fs, fs), :] = sums[t]

        groups(Z, 4, lambda ds: gather_sections([2 * d + y for d in ds]))

        def take_sections(ds):
            ids = [2 * d + 1 - y for d in ds]
            for p in ids:
                x_arrival(p).wait_recv()
            gather_sections(ids)

        groups(Z, 2, take_sections)

        yt[h] = hid[...].astype(BF)

        part = yt.shape[1] // 2

        def y_part(q, c, i, to_r):
            ref = yt.at[q, pl.ds(c * part, part)]
            return remote(ref, ref, y_send.at[i], y_recv.at[2 * q + c], l, to_r)

        def y_copy(i):
            return y_part(h, lax.rem(i, 2), i, lax.rem(r + 2 * (i // 2), R))

        def y_arrival(d, c):
            return y_part(lax.rem(h + d, H), c, 2 * d + c, r)

        each(2 * H, lambda i: y_copy(i).start(), 2)
        signal(go, l, twin)

        def m_copy(d):
            s = lax.rem(l + d, L)
            return remote(tiles.at[s, pl.ds(meta_at, metas)], mrecv.at[l], m_send.at[d], m_recv.at[l], s, r)

        def m_arrival(d):
            p = lax.rem(l + d, L)
            return remote(mrecv.at[p], mrecv.at[p], m_send.at[d], m_recv.at[p], p, r)

        each(L, lambda d: m_copy(d).start(), 1)
        mrecv[l] = tiles[l, pl.ds(meta_at, metas), :]
        on_worker(lambda copy: copy.wait_send())

        def x_passed(i):
            @pl.when(within(i, 1))
            def _():
                x_pass(i).wait_send()

        each(Z - 1, x_passed)
        each(H, lambda d: each(sections, lambda j: t_copy(d, j, lax.rem(r + 2 * d, R)).wait_send()), 1)

        w_own = w[pl.ds(pl.multiple_of(h * fs, fs), fs), :]
        for t in range(nt):
            if 2 * t % nt == 0:
                each(H, lambda d: y_arrival(d, 2 * t // nt).wait_recv(), 1)
            whole = jnp.concatenate([yt[q, pl.ds(t * fs, fs), :] for q in range(H)], axis=0)
            pre = dot(wt[...], whole, NN) + biasb[...]
            sig = 0.5 + 0.5 * jnp.tanh(0.5 * pre)
            act_t[t] = (pre * sig).astype(BF)
            g = (cot_t[t].astype(F32) * sig * (1.0 + pre * (1.0 - sig))).astype(BF)
            grad[t] = g
            hid[pl.ds(t * fs, fs), :] = dot(w_own, g, NN)

        def q_copy(i):
            s = other(i)
            return remote(psend.at[s], precv.at[l], q_send.at[i], q_recv.at[l], s, r)

        def q_arrival(i):
            p = nearest(i)
            return remote(precv.at[p], precv.at[p], q_send.at[i], q_recv.at[p], p, r)

        def products(s, out, at):
            meta = tiles[s, pl.ds(meta_at, metas), :].astype(F32)
            blocks = [hid[pl.ds(t * fs, fs), :] for t in range(nt)]
            for k in range(slots):
                base = 2 * nt * k
                picked = sum(
                    meta[base + t:base + t + 1, :] * blocks[t] for t in range(nt)
                ).astype(BF)
                out[at, pl.ds(k * fs, fs), :] = dot(
                    picked, tiles[s, pl.ds(k * tile, tile), :], NN).astype(BF)

        def send_products(ds):
            for d in ds:
                products(other(d), psend, other(d))
            for d in ds:
                q_copy(d).start()

        def w_copy(i):
            s = other(i)
            return remote(wsend.at[s], wrecv.at[l], w_send, w_recv, s, r)

        w_all = remote(wrecv.at[pl.ds(0, L - 1)], wrecv.at[pl.ds(0, L - 1)], w_send, w_recv, l, r)

        def rows_of(value):
            if rp < pad:
                value = jnp.concatenate([value, jnp.zeros((pad - rp, tile), F32)], axis=0)
            return value.astype(BF)

        gw = dot(
            jnp.concatenate([jnp.concatenate([yt[q, pl.ds(t * fs, fs), :] for q in range(H)], axis=0)
                             for t in range(nt)], axis=1),
            jnp.concatenate([grad[t] for t in range(nt)], axis=1), NT)
        for p in range(L):
            for i in range(2):
                wsend[p, pl.ds(i * pad, pad), :] = rows_of(
                    gw[p * rp:(p + 1) * rp, i * tile:(i + 1) * tile])
        each(L - 1, lambda i: w_copy(L - 2 - i).start())
        groups(L - 1, 4, send_products)
        ones = jnp.ones((metas, tile), BF)
        gb = sum(dot(ones, grad[t], NT) for t in range(nt))
        edge = lax.broadcasted_iota(jnp.int32, (metas, tile), 0)
        gb_rows = jnp.where(edge == 0, gb[:, :tile], jnp.where(edge == 1, gb[:, tile:], 0.0))
        wfin[l, pl.ds(2 * pad, metas), :] = gb_rows.astype(BF)
        wrecv[l] = wsend[l]
        products(l, precv, l)

        for t in range(nt):
            act_o[pl.ds(t * tile, tile), :] = flip(act_t[t])
        act_copy.start()

        each(L, lambda d: m_arrival(d).wait_recv(), 1)
        each(L, lambda d: m_copy(d).wait_send(), 1)
        each(2 * H, lambda i: y_copy(i).wait_send(), 2)
        pl.semaphore_wait(ready, L)

        w_all.wait_recv()
        total = wrecv[0].astype(F32)
        for p in range(1, L):
            total = total + wrecv[p].astype(F32)
        wfin[l, pl.ds(0, 2 * pad), :] = (total * grad_scale).astype(BF)

        def f_copy(d):
            return remote(wfin.at[l], wfin.at[l], f_send, f_recv, other(d), r)

        def e_copy(d):
            return remote(wfin.at[l], wfin.at[l], e_send, f_recv, d, twin)

        def give(i):
            e_copy(other(i)).start()
            f_copy(i).start()

        each(L - 1, give)
        e_copy(l).start()

        def add_products(ids):
            sums = [hid[pl.ds(c * fs, fs), :] for c in range(nt)]
            for p in ids:
                meta = mrecv[p].astype(F32)
                for k in range(slots):
                    part = precv[p, pl.ds(k * fs, fs), :].astype(F32)
                    for c in range(nt):
                        at = 2 * nt * k + nt + c
                        sums[c] = sums[c] + meta[at:at + 1, :] * part
            for c in range(nt):
                hid[pl.ds(c * fs, fs), :] = sums[c]

        def take_products(ds):
            for d in ds:
                q_arrival(d).wait_recv()
            add_products([nearest(d) for d in ds])

        add_products([l])
        groups(L - 1, 2, take_products)
        gft[h] = hid[...].astype(BF)
        each(H, lambda d: g_copy(d, lax.rem(twin + 2 * (H - 1 - d), R)).start())
        each(H, lambda d: g_copy(H - 1 + d, lax.rem(r + 2 * d, R)).start(), 1)

        act_copy.wait_send()
        each(L - 1, lambda i: q_copy(i).wait_send())
        w_all.wait_send()

        each(H, lambda d: g_arrival(lax.rem(h + d, H)).wait_recv(), 1)
        put_gf()
        f_some.wait_recv()
        put_gw()

        each(2 * H - 1, lambda d: g_copy(d, twin).wait_send())
        f_all.wait_send()
        f_some.wait_send()


def write_kernel(*refs):
    n = (len(refs) - 1) // 2
    copies = [pltpu.make_async_copy(refs[i], refs[n + i], refs[-1].at[i]) for i in range(n)]
    for copy in copies:
        copy.start()
    for copy in copies:
        copy.wait()


def write_out(*arrays):
    n = len(arrays)
    return pl.pallas_call(
        write_kernel,
        out_shape=tuple(jax.ShapeDtypeStruct(a.shape, a.dtype) for a in arrays),
        in_specs=[pl.BlockSpec(memory_space=pltpu.VMEM)] * n,
        out_specs=(pl.BlockSpec(memory_space=pltpu.HBM),) * n,
        scratch_shapes=[pltpu.SemaphoreType.DMA((n,))],
        name="write_out",
    )(*[pltpu.with_memory_space_constraint(a, pltpu.VMEM) for a in arrays])


def local(features, weight, out_bias, tile_values, tile_rows, tile_cols, tile_counts, cotangent):
    L, R = lax.axis_size("layer"), lax.axis_size("rep")
    H = R // 2
    rows_dev, hidden = cotangent.shape
    f_in = features.shape[1]
    _, sections, slots, tile, _ = tile_values.shape
    nt = rows_dev // tile
    fs = f_in // H
    metas = slots * 2 * nt
    pad = -(-(f_in // L) // 16) * 16
    vmem = pl.BlockSpec(memory_space=pltpu.VMEM)
    hbm = pl.BlockSpec(memory_space=pltpu.HBM)
    sem = pltpu.SemaphoreType.DMA
    regular = pltpu.SemaphoreType.REGULAR
    grad_scale = 1.0 / math.sqrt(rows_dev * L)
    act, gf, gw, gb = pl.pallas_call(
        functools.partial(kernel, L, R, grad_scale),
        out_shape=(
            jax.ShapeDtypeStruct((rows_dev, hidden), BF),
            jax.ShapeDtypeStruct((rows_dev, f_in), BF),
            jax.ShapeDtypeStruct((f_in, hidden), F32),
            jax.ShapeDtypeStruct((1, hidden), F32),
        ),
        in_specs=[hbm] * 8,
        out_specs=(vmem, vmem, vmem, vmem),
        scratch_shapes=[
            pltpu.VMEM(features.shape, BF),
            pltpu.VMEM(weight.shape, BF),
            pltpu.VMEM((1, hidden), F32),
            pltpu.SMEM(tile_rows.shape, jnp.int32),
            pltpu.SMEM(tile_rows.shape, jnp.int32),
            pltpu.SMEM(tile_rows.shape, jnp.int32),
            pltpu.VMEM(cotangent.shape, BF),
            sem((8,)),
            pltpu.VMEM((L, slots * tile + metas, tile), BF),
            pltpu.VMEM((L, nt * fs, tile), BF),
            pltpu.VMEM((H, nt * fs, tile), BF),
            pltpu.VMEM((hidden, f_in), BF),
            pltpu.VMEM((hidden, tile), F32),
            pltpu.VMEM((nt, hidden, tile), BF),
            pltpu.VMEM((nt, hidden, tile), BF),
            pltpu.VMEM((nt, hidden, tile), BF),
            pltpu.VMEM((nt * fs, tile), F32),
            pltpu.VMEM((L, slots * fs, tile), BF),
            pltpu.VMEM((L, slots * fs, tile), BF),
            pltpu.VMEM((L, metas, tile), BF),
            pltpu.VMEM((L, 2 * pad, tile), BF),
            pltpu.VMEM((L, 2 * pad, tile), BF),
            pltpu.VMEM((L, 2 * pad + metas, tile), BF),
            pltpu.VMEM((H, nt * fs, tile), BF),
            sem((H * sections,)), sem((L,)),
            sem((L,)), sem((L,)), sem((L,)),
            sem((2 * H,)), sem((2 * H,)),
            sem((L,)), sem((L,)),
            sem((L,)), sem((L,)),
            sem, sem,
            sem, sem, sem,
            sem((R,)), sem((H,)),
            sem, sem,
            regular, regular,
        ],
        compiler_params=pltpu.CompilerParams(
            collective_id=0, has_side_effects=True, vmem_limit_bytes=32 * 1024 * 1024
        ),
        name="graph_layer",
    )(*[pltpu.with_memory_space_constraint(x, pltpu.HBM) for x in (
        features, weight, out_bias.reshape(1, hidden),
        tile_values.reshape(sections, slots * tile, tile), tile_rows, tile_cols,
        tile_counts, cotangent)])
    return write_out(act, gf, gw, gb.reshape(hidden))


def solution(mesh):
    in_specs = (
        P("layer", None),
        P(),
        P(),
        P("layer", "rep", None, None, None),
        P("layer", "rep", None),
        P("layer", "rep", None),
        P("layer", "rep", None),
        P("layer", None),
    )
    out_specs = (P("layer", None), P("layer", None), P(), P())
    return jax.shard_map(local, mesh=mesh, in_specs=in_specs, out_specs=out_specs, check_vma=False)
```

```python
import functools
import math

import jax
import jax.numpy as jnp
from jax import lax
from jax.experimental import pallas as pl
from jax.experimental.pallas import tpu as pltpu
from jax.sharding import PartitionSpec as P

BF = jnp.bfloat16
F32 = jnp.float32
NT = (((1,), (1,)), ((), ()))
NN = (((1,), (0,)), ((), ()))
MESH = pl.DeviceIdType.MESH


def dot(a, b, dims):
    return lax.dot_general(a, b, dims, preferred_element_type=F32)


def flip(value):
    size = value.shape[1]
    eye = (lax.broadcasted_iota(jnp.int32, (size, size), 0)
           == lax.broadcasted_iota(jnp.int32, (size, size), 1))
    return dot(jnp.where(eye, 1.0, 0.0).astype(BF), value, NT).astype(BF)


def kernel(
    L, R, grad_scale,
    feat_h, w_h, bias_h, tv_h, rows_h, cols_h, counts_h, cot_h,
    act_o, gf_o, gw_o, gb_o,
    feat, w, bias, rows, cols, counts, cot, in_sem,
    tiles, xt, yt, wt, biasb, cot_t, act_t, grad, hid, psend, precv, mrecv, wsend, wrecv, wfin, gft,
    t_send, t_recv, x_send, x_fwd, x_recv, y_send, y_recv, m_send, m_recv,
    q_send, q_recv, w_send, w_recv, f_send, e_send, f_recv, g_send, g_recv, a_send, a_recv, go, ready,
):
    l = lax.axis_index("layer")
    r = lax.axis_index("rep")
    H = R // 2
    h = r // 2
    Z = L // 2
    z = l // 2
    y = lax.rem(l, 2)
    twin_l = l + 1 - 2 * y
    works_r = 2 * h + 1
    works = lax.rem(r, 2) == 1
    twin = r + 1 - 2 * lax.rem(r, 2)
    tile = tiles.shape[2]
    sections = counts.shape[1]
    slots = counts.shape[2]
    f_in, hidden = w.shape
    fs = f_in // H
    nt = feat.shape[0] // tile
    meta_at = slots * tile
    metas = tiles.shape[1] - meta_at
    rp = f_in // L
    pad = wsend.shape[1] // 2

    def remote(src, dst, ssem, rsem, to_l, to_r):
        return pltpu.make_async_remote_copy(
            src_ref=src, dst_ref=dst, send_sem=ssem, recv_sem=rsem,
            device_id={"layer": to_l, "rep": to_r}, device_id_type=MESH,
        )

    def signal(sem, to_l, to_r):
        pl.semaphore_signal(sem, inc=1, device_id={"layer": to_l, "rep": to_r}, device_id_type=MESH)

    def each(n, fn, start=0):
        lax.fori_loop(start, n, lambda i, c: (fn(i), c)[1], 0)

    def groups(n, size, fn, start=0):
        if n <= 8:
            for i in range(start, n, size):
                fn(list(range(i, min(i + size, n))))
        else:
            each(n, lambda i: fn([i]), start)

    def other(i):
        return i + jnp.where(i >= l, 1, 0)

    def nearest(i):
        return other(jnp.where(2 * l < L, i, L - 2 - i))

    barrier = pltpu.get_barrier_semaphore()
    meta_loads = [
        pltpu.make_async_copy(src, dst, in_sem.at[i])
        for i, (src, dst) in enumerate((
            (counts_h, counts), (rows_h, rows), (cols_h, cols), (feat_h, feat),
            (tv_h, tiles.at[pl.ds(r * sections, sections), pl.ds(0, meta_at)])))
    ]
    work_loads = [
        pltpu.make_async_copy(src, dst, in_sem.at[5 + i])
        for i, (src, dst) in enumerate(((w_h, w), (bias_h, bias), (cot_h, cot)))
    ]
    meta_loads[3].start()

    @pl.when(works)
    def _():
        each(L, lambda d: signal(barrier, lax.rem(l + d, L), r), 1)
        each(L, lambda d: signal(barrier, lax.rem(l + d, L), twin), 1)
        each(H, lambda d: signal(barrier, l, lax.rem(r + 2 * d, R)), 1)

    each(H, lambda d: signal(barrier, l, lax.rem(twin + 2 * d, R)))
    for load in meta_loads[:3] + meta_loads[4:]:
        load.start()

    @pl.when(works)
    def _():
        for load in work_loads:
            load.start()

    meta_loads[3].wait()
    pick = (lax.broadcasted_iota(jnp.int32, (fs, f_in), 1)
            == h * fs + lax.broadcasted_iota(jnp.int32, (fs, f_in), 0))
    own = dot(jnp.where(pick, 1.0, 0.0).astype(BF), feat[...], NT).astype(BF)
    for t in range(nt):
        xt[l, pl.ds(t * fs, fs), :] = own[:, t * tile:(t + 1) * tile]

    def pair(i):
        i = jnp.where(2 * z < Z, i, Z - 2 - i)
        return i + jnp.where(i >= z, 1, 0)

    def x_copy(i, p, to_r):
        return remote(xt.at[l], xt.at[l], x_send.at[i], x_recv.at[l], p, to_r)

    def x_same(i):
        return x_copy(2 * i, 2 * pair(i) + y, works_r)

    def x_cross(i):
        return x_copy(2 * i + 1, 2 * pair(i) + 1 - y, works_r)

    def passed_there(i):
        there = pair(i)
        k = z - jnp.where(z > there, 1, 0)
        k = jnp.where(2 * there < Z, k, Z - 2 - k)
        return (k < 2) & (z < there + 2)

    def passes(i):
        return (i < 2) & (pair(i) < z + 2)

    def x_pass(i):
        p = 2 * pair(i) + y
        return remote(xt.at[p], xt.at[p], x_fwd.at[i], x_recv.at[p], twin_l, r)

    def on_worker(do):
        each(Z - 1, lambda i: do(x_same(i)))

    def on_other(do):
        do(x_twin())

        def visit(i):
            @pl.when(jnp.logical_not(passed_there(i)))
            def _():
                do(x_cross(i))

        each(Z - 1, visit)

    def x_twin():
        return x_copy(L - 1, twin_l, works_r)

    def x_arrival(p):
        return remote(xt.at[p], xt.at[p], x_send.at[0], x_recv.at[p], p, r)

    def t_copy(d, j, to_r):
        s = r * sections + j
        return remote(tiles.at[s], tiles.at[s], t_send.at[d * sections + j], t_recv.at[s], l, to_r)

    def t_arrival(q, j):
        s = lax.rem(q, R) * sections + j
        return remote(tiles.at[s], tiles.at[s], t_send.at[0], t_recv.at[s], l, r)

    def g_copy(d, to_r):
        return remote(gft.at[h], gft.at[h], g_send.at[d], g_recv.at[h], l, to_r)

    def g_arrival(q):
        return remote(gft.at[q], gft.at[q], g_send.at[0], g_recv.at[q], l, r)

    f_some = remote(wfin.at[pl.ds(0, L - 1)], wfin.at[pl.ds(0, L - 1)], f_send, f_recv, l, r)
    f_all = remote(wfin, wfin, e_send, f_recv, l, r)

    def put_metas():
        for load in meta_loads[:3]:
            load.wait()
        lanes = lax.broadcasted_iota(jnp.int32, (metas, tile), 1)
        row_ids = lax.broadcasted_iota(jnp.int32, (metas, tile), 0)
        for j in range(sections):
            meta = jnp.zeros((metas, tile), F32)
            for k in range(slots):
                base = 2 * nt * k
                meta = meta + jnp.where(row_ids == base + rows[0, j, k], 1.0, 0.0)
                live = jnp.where(lanes < counts[0, j, k], 1.0, 0.0)
                meta = meta + jnp.where(row_ids == base + nt + cols[0, j, k], live, 0.0)
            tiles[r * sections + j, pl.ds(meta_at, metas), :] = meta.astype(BF)

    act_copy = remote(act_o, act_o, a_send, a_recv, l, twin)

    def put_gf():
        for t in range(nt):
            whole = jnp.concatenate([gft[q, pl.ds(t * fs, fs), :] for q in range(H)], axis=0)
            gf_o[pl.ds(t * tile, tile), :] = flip(whole)

    def put_gw():
        total = jnp.zeros((metas, tile), F32)
        for p in range(L):
            total = total + wfin[p, pl.ds(2 * pad, metas), :].astype(F32)
            for i in range(2):
                gw_o[pl.ds(p * rp, rp), pl.ds(i * tile, tile)] = (
                    wfin[p, pl.ds(i * pad, pad), :].astype(F32)[:rp])
        total = total * grad_scale
        for i in range(2):
            gb_o[:, pl.ds(i * tile, tile)] = total[i:i + 1]

    @pl.when(jnp.logical_not(works))
    def _():
        pl.semaphore_wait(barrier, H + L - 1)

        def send(d):
            each(sections, lambda j: t_copy(d, j, lax.rem(twin + 2 * d, R)).start())

        on_other(lambda copy: copy.start())
        put_metas()
        meta_loads[4].wait()
        each(H, lambda d: send(H - 1 - d))
        pl.semaphore_wait(go, 1)
        each(L, lambda d: signal(ready, lax.rem(l + d, L), twin))
        each(H, lambda d: each(sections, lambda j: t_copy(d, j, lax.rem(twin + 2 * d, R)).wait_send()))
        on_other(lambda copy: copy.wait_send())
        act_copy.wait_recv()
        each(H, lambda q: g_arrival(q).wait_recv())
        put_gf()
        f_all.wait_recv()
        put_gw()

    @pl.when(works)
    def _():
        pl.semaphore_wait(barrier, L - 1 + H - 1 + H)

        on_worker(lambda copy: copy.start())
        put_metas()
        meta_loads[4].wait()
        each(H, lambda d: each(sections, lambda j: t_copy(d, j, lax.rem(r + 2 * d, R)).start()), 1)

        for load in work_loads:
            load.wait()
        wt[...] = flip(w[...])
        biasb[...] = jnp.transpose(jnp.broadcast_to(bias[...], (tile, hidden)), (1, 0))
        for t in range(nt):
            cot_t[t] = flip(cot[pl.ds(t * tile, tile), :])
        hid[...] = xt[l].astype(F32)

        def x_take(i):
            x_pass(i).wait_recv()

            @pl.when(passes(i))
            def _():
                x_pass(i).start()

        each(Z - 1, x_take)
        each(H, lambda d: each(sections, lambda j: t_arrival(twin + 2 * d, j).wait_recv()))
        each(H, lambda d: each(sections, lambda j: t_arrival(r + 2 * d, j).wait_recv()), 1)

        def gather_sections(ids):
            sums = [hid[pl.ds(t * fs, fs), :] for t in range(nt)]
            for s in ids:
                meta = tiles[s, pl.ds(meta_at, metas), :].astype(F32)
                blocks = [xt[s, pl.ds(c * fs, fs), :].astype(F32) for c in range(nt)]
                for k in range(slots):
                    base = 2 * nt * k
                    picked = sum(
                        meta[base + nt + c:base + nt + c + 1, :] * blocks[c] for c in range(nt)
                    ).astype(BF)
                    product = dot(picked, tiles[s, pl.ds(k * tile, tile), :], NT)
                    for t in range(nt):
                        sums[t] = sums[t] + meta[base + t:base + t + 1, :] * product
            for t in range(nt):
                hid[pl.ds(t * fs, fs), :] = sums[t]

        groups(Z, 4, lambda ds: gather_sections([2 * d + y for d in ds]))

        def take_sections(ds):
            ids = [2 * d + 1 - y for d in ds]
            for p in ids:
                x_arrival(p).wait_recv()
            gather_sections(ids)

        groups(Z, 2, take_sections)

        yt[h] = hid[...].astype(BF)

        part = yt.shape[1] // 2

        def y_part(q, c, i, to_r):
            ref = yt.at[q, pl.ds(c * part, part)]
            return remote(ref, ref, y_send.at[i], y_recv.at[2 * q + c], l, to_r)

        def y_copy(i):
            return y_part(h, lax.rem(i, 2), i, lax.rem(r + 2 * (i // 2), R))

        def y_arrival(d, c):
            return y_part(lax.rem(h + d, H), c, 2 * d + c, r)

        each(2 * H, lambda i: y_copy(i).start(), 2)
        signal(go, l, twin)

        def m_copy(d):
            s = lax.rem(l + d, L)
            return remote(tiles.at[s, pl.ds(meta_at, metas)], mrecv.at[l], m_send.at[d], m_recv.at[l], s, r)

        def m_arrival(d):
            p = lax.rem(l + d, L)
            return remote(mrecv.at[p], mrecv.at[p], m_send.at[d], m_recv.at[p], p, r)

        each(L, lambda d: m_copy(d).start(), 1)
        mrecv[l] = tiles[l, pl.ds(meta_at, metas), :]
        on_worker(lambda copy: copy.wait_send())

        def x_passed(i):
            @pl.when(passes(i))
            def _():
                x_pass(i).wait_send()

        each(Z - 1, x_passed)
        each(H, lambda d: each(sections, lambda j: t_copy(d, j, lax.rem(r + 2 * d, R)).wait_send()), 1)

        w_own = w[pl.ds(pl.multiple_of(h * fs, fs), fs), :]
        for t in range(nt):
            if 2 * t % nt == 0:
                each(H, lambda d: y_arrival(d, 2 * t // nt).wait_recv(), 1)
            whole = jnp.concatenate([yt[q, pl.ds(t * fs, fs), :] for q in range(H)], axis=0)
            pre = dot(wt[...], whole, NN) + biasb[...]
            sig = 0.5 + 0.5 * jnp.tanh(0.5 * pre)
            act_t[t] = (pre * sig).astype(BF)
            g = (cot_t[t].astype(F32) * sig * (1.0 + pre * (1.0 - sig))).astype(BF)
            grad[t] = g
            hid[pl.ds(t * fs, fs), :] = dot(w_own, g, NN)

        def q_copy(i):
            s = other(i)
            return remote(psend.at[s], precv.at[l], q_send.at[i], q_recv.at[l], s, r)

        def q_arrival(i):
            p = nearest(i)
            return remote(precv.at[p], precv.at[p], q_send.at[i], q_recv.at[p], p, r)

        def products(s, out, at):
            meta = tiles[s, pl.ds(meta_at, metas), :].astype(F32)
            blocks = [hid[pl.ds(t * fs, fs), :] for t in range(nt)]
            for k in range(slots):
                base = 2 * nt * k
                picked = sum(
                    meta[base + t:base + t + 1, :] * blocks[t] for t in range(nt)
                ).astype(BF)
                out[at, pl.ds(k * fs, fs), :] = dot(
                    picked, tiles[s, pl.ds(k * tile, tile), :], NN).astype(BF)

        def send_products(ds):
            for d in ds:
                products(other(d), psend, other(d))
            for d in ds:
                q_copy(d).start()

        def w_copy(i):
            s = other(i)
            return remote(wsend.at[s], wrecv.at[l], w_send, w_recv, s, r)

        w_all = remote(wrecv.at[pl.ds(0, L - 1)], wrecv.at[pl.ds(0, L - 1)], w_send, w_recv, l, r)

        def rows_of(value):
            if rp < pad:
                value = jnp.concatenate([value, jnp.zeros((pad - rp, tile), F32)], axis=0)
            return value.astype(BF)

        gw = dot(
            jnp.concatenate([jnp.concatenate([yt[q, pl.ds(t * fs, fs), :] for q in range(H)], axis=0)
                             for t in range(nt)], axis=1),
            jnp.concatenate([grad[t] for t in range(nt)], axis=1), NT)
        for p in range(L):
            for i in range(2):
                wsend[p, pl.ds(i * pad, pad), :] = rows_of(
                    gw[p * rp:(p + 1) * rp, i * tile:(i + 1) * tile])
        each(L - 1, lambda i: w_copy(L - 2 - i).start())
        groups(L - 1, 4, send_products)
        ones = jnp.ones((metas, tile), BF)
        gb = sum(dot(ones, grad[t], NT) for t in range(nt))
        edge = lax.broadcasted_iota(jnp.int32, (metas, tile), 0)
        gb_rows = jnp.where(edge == 0, gb[:, :tile], jnp.where(edge == 1, gb[:, tile:], 0.0))
        wfin[l, pl.ds(2 * pad, metas), :] = gb_rows.astype(BF)
        wrecv[l] = wsend[l]
        products(l, precv, l)

        for t in range(nt):
            act_o[pl.ds(t * tile, tile), :] = flip(act_t[t])
        act_copy.start()

        each(L, lambda d: m_arrival(d).wait_recv(), 1)
        each(L, lambda d: m_copy(d).wait_send(), 1)
        each(2 * H, lambda i: y_copy(i).wait_send(), 2)
        pl.semaphore_wait(ready, L)

        w_all.wait_recv()
        total = wrecv[0].astype(F32)
        for p in range(1, L):
            total = total + wrecv[p].astype(F32)
        wfin[l, pl.ds(0, 2 * pad), :] = (total * grad_scale).astype(BF)

        def f_copy(d):
            return remote(wfin.at[l], wfin.at[l], f_send, f_recv, other(d), r)

        def e_copy(d):
            return remote(wfin.at[l], wfin.at[l], e_send, f_recv, d, twin)

        def give(i):
            e_copy(other(i)).start()
            f_copy(i).start()

        each(L - 1, give)
        e_copy(l).start()

        def add_products(ids):
            sums = [hid[pl.ds(c * fs, fs), :] for c in range(nt)]
            for p in ids:
                meta = mrecv[p].astype(F32)
                for k in range(slots):
                    part = precv[p, pl.ds(k * fs, fs), :].astype(F32)
                    for c in range(nt):
                        at = 2 * nt * k + nt + c
                        sums[c] = sums[c] + meta[at:at + 1, :] * part
            for c in range(nt):
                hid[pl.ds(c * fs, fs), :] = sums[c]

        def take_products(ds):
            for d in ds:
                q_arrival(d).wait_recv()
            add_products([nearest(d) for d in ds])

        add_products([l])
        groups(L - 1, 2, take_products)
        gft[h] = hid[...].astype(BF)
        each(H, lambda d: g_copy(d, lax.rem(twin + 2 * (H - 1 - d), R)).start())
        each(H, lambda d: g_copy(H - 1 + d, lax.rem(r + 2 * d, R)).start(), 1)

        act_copy.wait_send()
        each(L - 1, lambda i: q_copy(i).wait_send())
        w_all.wait_send()

        each(H, lambda d: g_arrival(lax.rem(h + d, H)).wait_recv(), 1)
        put_gf()
        f_some.wait_recv()
        put_gw()

        each(2 * H - 1, lambda d: g_copy(d, twin).wait_send())
        f_all.wait_send()
        f_some.wait_send()


def write_kernel(*refs):
    n = (len(refs) - 1) // 2
    copies = [pltpu.make_async_copy(refs[i], refs[n + i], refs[-1].at[i]) for i in range(n)]
    for copy in copies:
        copy.start()
    for copy in copies:
        copy.wait()


def write_out(*arrays):
    n = len(arrays)
    return pl.pallas_call(
        write_kernel,
        out_shape=tuple(jax.ShapeDtypeStruct(a.shape, a.dtype) for a in arrays),
        in_specs=[pl.BlockSpec(memory_space=pltpu.VMEM)] * n,
        out_specs=(pl.BlockSpec(memory_space=pltpu.HBM),) * n,
        scratch_shapes=[pltpu.SemaphoreType.DMA((n,))],
        name="write_out",
    )(*[pltpu.with_memory_space_constraint(a, pltpu.VMEM) for a in arrays])


def local(features, weight, out_bias, tile_values, tile_rows, tile_cols, tile_counts, cotangent):
    L, R = lax.axis_size("layer"), lax.axis_size("rep")
    H = R // 2
    rows_dev, hidden = cotangent.shape
    f_in = features.shape[1]
    _, sections, slots, tile, _ = tile_values.shape
    nt = rows_dev // tile
    fs = f_in // H
    metas = slots * 2 * nt
    pad = -(-(f_in // L) // 16) * 16
    vmem = pl.BlockSpec(memory_space=pltpu.VMEM)
    hbm = pl.BlockSpec(memory_space=pltpu.HBM)
    sem = pltpu.SemaphoreType.DMA
    regular = pltpu.SemaphoreType.REGULAR
    grad_scale = 1.0 / math.sqrt(rows_dev * L)
    act, gf, gw, gb = pl.pallas_call(
        functools.partial(kernel, L, R, grad_scale),
        out_shape=(
            jax.ShapeDtypeStruct((rows_dev, hidden), BF),
            jax.ShapeDtypeStruct((rows_dev, f_in), BF),
            jax.ShapeDtypeStruct((f_in, hidden), F32),
            jax.ShapeDtypeStruct((1, hidden), F32),
        ),
        in_specs=[hbm] * 8,
        out_specs=(vmem, vmem, vmem, vmem),
        scratch_shapes=[
            pltpu.VMEM(features.shape, BF),
            pltpu.VMEM(weight.shape, BF),
            pltpu.VMEM((1, hidden), F32),
            pltpu.SMEM(tile_rows.shape, jnp.int32),
            pltpu.SMEM(tile_rows.shape, jnp.int32),
            pltpu.SMEM(tile_rows.shape, jnp.int32),
            pltpu.VMEM(cotangent.shape, BF),
            sem((8,)),
            pltpu.VMEM((L, slots * tile + metas, tile), BF),
            pltpu.VMEM((L, nt * fs, tile), BF),
            pltpu.VMEM((H, nt * fs, tile), BF),
            pltpu.VMEM((hidden, f_in), BF),
            pltpu.VMEM((hidden, tile), F32),
            pltpu.VMEM((nt, hidden, tile), BF),
            pltpu.VMEM((nt, hidden, tile), BF),
            pltpu.VMEM((nt, hidden, tile), BF),
            pltpu.VMEM((nt * fs, tile), F32),
            pltpu.VMEM((L, slots * fs, tile), BF),
            pltpu.VMEM((L, slots * fs, tile), BF),
            pltpu.VMEM((L, metas, tile), BF),
            pltpu.VMEM((L, 2 * pad, tile), BF),
            pltpu.VMEM((L, 2 * pad, tile), BF),
            pltpu.VMEM((L, 2 * pad + metas, tile), BF),
            pltpu.VMEM((H, nt * fs, tile), BF),
            sem((H * sections,)), sem((L,)),
            sem((L,)), sem((L,)), sem((L,)),
            sem((2 * H,)), sem((2 * H,)),
            sem((L,)), sem((L,)),
            sem((L,)), sem((L,)),
            sem, sem,
            sem, sem, sem,
            sem((R,)), sem((H,)),
            sem, sem,
            regular, regular,
        ],
        compiler_params=pltpu.CompilerParams(
            collective_id=0, has_side_effects=True, vmem_limit_bytes=32 * 1024 * 1024
        ),
        name="graph_layer",
    )(*[pltpu.with_memory_space_constraint(x, pltpu.HBM) for x in (
        features, weight, out_bias.reshape(1, hidden),
        tile_values.reshape(sections, slots * tile, tile), tile_rows, tile_cols,
        tile_counts, cotangent)])
    return write_out(act, gf, gw, gb.reshape(hidden))


def solution(mesh):
    in_specs = (
        P("layer", None),
        P(),
        P(),
        P("layer", "rep", None, None, None),
        P("layer", "rep", None),
        P("layer", "rep", None),
        P("layer", "rep", None),
        P("layer", None),
    )
    out_specs = (P("layer", None), P("layer", None), P(), P())
    return jax.shard_map(local, mesh=mesh, in_specs=in_specs, out_specs=out_specs, check_vma=False)
```

```python
import functools
import math

import jax
import jax.numpy as jnp
from jax import lax
from jax.experimental import pallas as pl
from jax.experimental.pallas import tpu as pltpu
from jax.sharding import PartitionSpec as P

BF = jnp.bfloat16
F32 = jnp.float32
NT = (((1,), (1,)), ((), ()))
NN = (((1,), (0,)), ((), ()))
MESH = pl.DeviceIdType.MESH


def dot(a, b, dims):
    return lax.dot_general(a, b, dims, preferred_element_type=F32)


def flip(value):
    size = value.shape[1]
    eye = (lax.broadcasted_iota(jnp.int32, (size, size), 0)
           == lax.broadcasted_iota(jnp.int32, (size, size), 1))
    return dot(jnp.where(eye, 1.0, 0.0).astype(BF), value, NT).astype(BF)


def kernel(
    L, R, grad_scale,
    feat_h, w_h, bias_h, tv_h, rows_h, cols_h, counts_h, cot_h,
    act_o, gf_o, gw_o, gb_o,
    feat, w, bias, rows, cols, counts, cot, in_sem,
    tiles, xt, yt, wt, biasb, cot_t, act_t, grad, hid, psend, precv, mrecv, wsend, wrecv, wfin, gft,
    t_send, t_recv, x_send, x_fwd, x_recv, y_send, y_recv, m_send, m_recv,
    q_send, q_recv, w_send, w_recv, f_send, e_send, f_recv, g_send, g_recv, a_send, a_recv, go, ready,
):
    l = lax.axis_index("layer")
    r = lax.axis_index("rep")
    H = R // 2
    h = r // 2
    Z = L // 2
    z = l // 2
    y = lax.rem(l, 2)
    twin_l = l + 1 - 2 * y
    works_r = 2 * h + 1
    works = lax.rem(r, 2) == 1
    twin = r + 1 - 2 * lax.rem(r, 2)
    tile = tiles.shape[2]
    sections = counts.shape[1]
    slots = counts.shape[2]
    f_in, hidden = w.shape
    fs = f_in // H
    nt = feat.shape[0] // tile
    meta_at = slots * tile
    metas = tiles.shape[1] - meta_at
    rp = f_in // L
    pad = wsend.shape[1] // 2

    def remote(src, dst, ssem, rsem, to_l, to_r):
        return pltpu.make_async_remote_copy(
            src_ref=src, dst_ref=dst, send_sem=ssem, recv_sem=rsem,
            device_id={"layer": to_l, "rep": to_r}, device_id_type=MESH,
        )

    def signal(sem, to_l, to_r):
        pl.semaphore_signal(sem, inc=1, device_id={"layer": to_l, "rep": to_r}, device_id_type=MESH)

    def each(n, fn, start=0):
        lax.fori_loop(start, n, lambda i, c: (fn(i), c)[1], 0)

    def groups(n, size, fn, start=0):
        if n <= 8:
            for i in range(start, n, size):
                fn(list(range(i, min(i + size, n))))
        else:
            each(n, lambda i: fn([i]), start)

    def other(i):
        return i + jnp.where(i >= l, 1, 0)

    def nearest(i):
        return other(jnp.where(2 * l < L, i, L - 2 - i))

    barrier = pltpu.get_barrier_semaphore()
    meta_loads = [
        pltpu.make_async_copy(src, dst, in_sem.at[i])
        for i, (src, dst) in enumerate((
            (counts_h, counts), (rows_h, rows), (cols_h, cols), (feat_h, feat),
            (tv_h, tiles.at[pl.ds(r * sections, sections), pl.ds(0, meta_at)])))
    ]
    work_loads = [
        pltpu.make_async_copy(src, dst, in_sem.at[5 + i])
        for i, (src, dst) in enumerate(((w_h, w), (bias_h, bias), (cot_h, cot)))
    ]
    meta_loads[3].start()

    @pl.when(works)
    def _():
        each(L, lambda d: signal(barrier, lax.rem(l + d, L), r), 1)
        each(L, lambda d: signal(barrier, lax.rem(l + d, L), twin), 1)
        each(H, lambda d: signal(barrier, l, lax.rem(r + 2 * d, R)), 1)

    each(H, lambda d: signal(barrier, l, lax.rem(twin + 2 * d, R)))
    for load in meta_loads[:3] + meta_loads[4:]:
        load.start()

    @pl.when(works)
    def _():
        for load in work_loads:
            load.start()

    meta_loads[3].wait()
    pick = (lax.broadcasted_iota(jnp.int32, (fs, f_in), 1)
            == h * fs + lax.broadcasted_iota(jnp.int32, (fs, f_in), 0))
    own = dot(jnp.where(pick, 1.0, 0.0).astype(BF), feat[...], NT).astype(BF)
    for t in range(nt):
        xt[l, pl.ds(t * fs, fs), :] = own[:, t * tile:(t + 1) * tile]

    def pair(i):
        i = jnp.where(2 * z < Z, i, Z - 2 - i)
        return i + jnp.where(i >= z, 1, 0)

    def x_copy(i, p, to_r):
        return remote(xt.at[l], xt.at[l], x_send.at[i], x_recv.at[l], p, to_r)

    def x_same(i):
        return x_copy(2 * i, 2 * pair(i) + y, works_r)

    def x_cross(i):
        return x_copy(2 * i + 1, 2 * pair(i) + 1 - y, works_r)

    def passed_there(i):
        there = pair(i)
        k = z - jnp.where(z > there, 1, 0)
        k = jnp.where(2 * there < Z, k, Z - 2 - k)
        return (k < 2) & (z < there + 2)

    def passes(i):
        return (i < 2) & (pair(i) < z + 2)

    def x_pass(i):
        p = 2 * pair(i) + y
        return remote(xt.at[p], xt.at[p], x_fwd.at[i], x_recv.at[p], twin_l, r)

    def on_worker(do):
        each(Z - 1, lambda i: do(x_same(i)))

    def on_other(do):
        do(x_twin())

        def visit(i):
            @pl.when(jnp.logical_not(passed_there(i)))
            def _():
                do(x_cross(i))

        each(Z - 1, visit)

    def x_twin():
        return x_copy(L - 1, twin_l, works_r)

    def x_arrival(p):
        return remote(xt.at[p], xt.at[p], x_send.at[0], x_recv.at[p], p, r)

    def t_copy(d, j, to_r):
        s = r * sections + j
        return remote(tiles.at[s], tiles.at[s], t_send.at[d * sections + j], t_recv.at[s], l, to_r)

    def t_arrival(q, j):
        s = lax.rem(q, R) * sections + j
        return remote(tiles.at[s], tiles.at[s], t_send.at[0], t_recv.at[s], l, r)

    def g_copy(d, to_r):
        return remote(gft.at[h], gft.at[h], g_send.at[d], g_recv.at[h], l, to_r)

    def g_arrival(q):
        return remote(gft.at[q], gft.at[q], g_send.at[0], g_recv.at[q], l, r)

    f_some = remote(wfin.at[pl.ds(0, L - 1)], wfin.at[pl.ds(0, L - 1)], f_send, f_recv, l, r)
    f_all = remote(wfin, wfin, e_send, f_recv, l, r)

    def put_metas():
        for load in meta_loads[:3]:
            load.wait()
        lanes = lax.broadcasted_iota(jnp.int32, (metas, tile), 1)
        row_ids = lax.broadcasted_iota(jnp.int32, (metas, tile), 0)
        for j in range(sections):
            meta = jnp.zeros((metas, tile), F32)
            for k in range(slots):
                base = 2 * nt * k
                meta = meta + jnp.where(row_ids == base + rows[0, j, k], 1.0, 0.0)
                live = jnp.where(lanes < counts[0, j, k], 1.0, 0.0)
                meta = meta + jnp.where(row_ids == base + nt + cols[0, j, k], live, 0.0)
            tiles[r * sections + j, pl.ds(meta_at, metas), :] = meta.astype(BF)

    act_copy = remote(act_o, act_o, a_send, a_recv, l, twin)

    def put_gf():
        for t in range(nt):
            whole = jnp.concatenate([gft[q, pl.ds(t * fs, fs), :] for q in range(H)], axis=0)
            gf_o[pl.ds(t * tile, tile), :] = flip(whole)

    def put_gw():
        total = jnp.zeros((metas, tile), F32)
        for p in range(L):
            total = total + wfin[p, pl.ds(2 * pad, metas), :].astype(F32)
            for i in range(2):
                gw_o[pl.ds(p * rp, rp), pl.ds(i * tile, tile)] = (
                    wfin[p, pl.ds(i * pad, pad), :].astype(F32)[:rp])
        total = total * grad_scale
        for i in range(2):
            gb_o[:, pl.ds(i * tile, tile)] = total[i:i + 1]

    @pl.when(jnp.logical_not(works))
    def _():
        pl.semaphore_wait(barrier, H + L - 1)

        def send(d):
            each(sections, lambda j: t_copy(d, j, lax.rem(twin + 2 * d, R)).start())

        on_other(lambda copy: copy.start())
        put_metas()
        meta_loads[4].wait()
        each(H, lambda d: send(H - 1 - d))
        pl.semaphore_wait(go, 1)
        each(L, lambda d: signal(ready, lax.rem(l + d, L), twin))
        each(H, lambda d: each(sections, lambda j: t_copy(d, j, lax.rem(twin + 2 * d, R)).wait_send()))
        on_other(lambda copy: copy.wait_send())
        act_copy.wait_recv()
        each(H, lambda q: g_arrival(q).wait_recv())
        put_gf()
        f_all.wait_recv()
        put_gw()

    @pl.when(works)
    def _():
        pl.semaphore_wait(barrier, L - 1 + H - 1 + H)

        on_worker(lambda copy: copy.start())
        put_metas()
        meta_loads[4].wait()
        each(H, lambda d: each(sections, lambda j: t_copy(d, j, lax.rem(r + 2 * d, R)).start()), 1)

        for load in work_loads:
            load.wait()
        wt[...] = flip(w[...])
        biasb[...] = jnp.transpose(jnp.broadcast_to(bias[...], (tile, hidden)), (1, 0))
        for t in range(nt):
            cot_t[t] = flip(cot[pl.ds(t * tile, tile), :])
        hid[...] = xt[l].astype(F32)

        def x_take(i):
            x_pass(i).wait_recv()

            @pl.when(passes(i))
            def _():
                x_pass(i).start()

        each(Z - 1, x_take)
        each(H, lambda d: each(sections, lambda j: t_arrival(twin + 2 * d, j).wait_recv()))
        each(H, lambda d: each(sections, lambda j: t_arrival(r + 2 * d, j).wait_recv()), 1)

        def gather_sections(ids):
            sums = [hid[pl.ds(t * fs, fs), :] for t in range(nt)]
            for s in ids:
                meta = tiles[s, pl.ds(meta_at, metas), :].astype(F32)
                blocks = [xt[s, pl.ds(c * fs, fs), :].astype(F32) for c in range(nt)]
                for k in range(slots):
                    base = 2 * nt * k
                    picked = sum(
                        meta[base + nt + c:base + nt + c + 1, :] * blocks[c] for c in range(nt)
                    ).astype(BF)
                    product = dot(picked, tiles[s, pl.ds(k * tile, tile), :], NT)
                    for t in range(nt):
                        sums[t] = sums[t] + meta[base + t:base + t + 1, :] * product
            for t in range(nt):
                hid[pl.ds(t * fs, fs), :] = sums[t]

        groups(Z, 4, lambda ds: gather_sections([2 * d + y for d in ds]))

        def take_sections(ds):
            ids = [2 * d + 1 - y for d in ds]
            for p in ids:
                x_arrival(p).wait_recv()
            gather_sections(ids)

        groups(Z, 2, take_sections)

        yt[h] = hid[...].astype(BF)

        part = yt.shape[1] // 2

        def y_part(q, c, i, to_r):
            ref = yt.at[q, pl.ds(c * part, part)]
            return remote(ref, ref, y_send.at[i], y_recv.at[2 * q + c], l, to_r)

        def y_copy(i):
            return y_part(h, lax.rem(i, 2), i, lax.rem(r + 2 * (i // 2), R))

        def y_arrival(d, c):
            return y_part(lax.rem(h + d, H), c, 2 * d + c, r)

        each(2 * H, lambda i: y_copy(i).start(), 2)
        signal(go, l, twin)

        def m_copy(d):
            s = lax.rem(l + d, L)
            return remote(tiles.at[s, pl.ds(meta_at, metas)], mrecv.at[l], m_send.at[d], m_recv.at[l], s, r)

        def m_arrival(d):
            p = lax.rem(l + d, L)
            return remote(mrecv.at[p], mrecv.at[p], m_send.at[d], m_recv.at[p], p, r)

        each(L, lambda d: m_copy(d).start(), 1)
        mrecv[l] = tiles[l, pl.ds(meta_at, metas), :]
        on_worker(lambda copy: copy.wait_send())

        def x_passed(i):
            @pl.when(passes(i))
            def _():
                x_pass(i).wait_send()

        each(Z - 1, x_passed)
        each(H, lambda d: each(sections, lambda j: t_copy(d, j, lax.rem(r + 2 * d, R)).wait_send()), 1)

        w_own = w[pl.ds(pl.multiple_of(h * fs, fs), fs), :]
        for t in range(nt):
            if 2 * t % nt == 0:
                each(H, lambda d: y_arrival(d, 2 * t // nt).wait_recv(), 1)
            whole = jnp.concatenate([yt[q, pl.ds(t * fs, fs), :] for q in range(H)], axis=0)
            pre = dot(wt[...], whole, NN) + biasb[...]
            sig = 0.5 + 0.5 * jnp.tanh(0.5 * pre)
            act_t[t] = (pre * sig).astype(BF)
            g = (cot_t[t].astype(F32) * sig * (1.0 + pre * (1.0 - sig))).astype(BF)
            grad[t] = g

        def q_copy(i):
            s = other(i)
            return remote(psend.at[s], precv.at[l], q_send.at[i], q_recv.at[l], s, r)

        def q_arrival(i):
            p = nearest(i)
            return remote(precv.at[p], precv.at[p], q_send.at[i], q_recv.at[p], p, r)

        def products(s, out, at):
            meta = tiles[s, pl.ds(meta_at, metas), :].astype(F32)
            blocks = [hid[pl.ds(t * fs, fs), :] for t in range(nt)]
            for k in range(slots):
                base = 2 * nt * k
                picked = sum(
                    meta[base + t:base + t + 1, :] * blocks[t] for t in range(nt)
                ).astype(BF)
                out[at, pl.ds(k * fs, fs), :] = dot(
                    picked, tiles[s, pl.ds(k * tile, tile), :], NN).astype(BF)

        def send_products(ds):
            for d in ds:
                products(other(d), psend, other(d))
            for d in ds:
                q_copy(d).start()

        def w_copy(i):
            s = other(i)
            return remote(wsend.at[s], wrecv.at[l], w_send, w_recv, s, r)

        w_all = remote(wrecv.at[pl.ds(0, L - 1)], wrecv.at[pl.ds(0, L - 1)], w_send, w_recv, l, r)

        def rows_of(value):
            if rp < pad:
                value = jnp.concatenate([value, jnp.zeros((pad - rp, tile), F32)], axis=0)
            return value.astype(BF)

        gw = dot(
            jnp.concatenate([jnp.concatenate([yt[q, pl.ds(t * fs, fs), :] for q in range(H)], axis=0)
                             for t in range(nt)], axis=1),
            jnp.concatenate([grad[t] for t in range(nt)], axis=1), NT)
        for p in range(L):
            for i in range(2):
                wsend[p, pl.ds(i * pad, pad), :] = rows_of(
                    gw[p * rp:(p + 1) * rp, i * tile:(i + 1) * tile])
        each(L - 1, lambda i: w_copy(L - 2 - i).start())
        for t in range(nt):
            hid[pl.ds(t * fs, fs), :] = dot(w_own, grad[t], NN)
        groups(L - 1, 4, send_products)
        ones = jnp.ones((metas, tile), BF)
        gb = sum(dot(ones, grad[t], NT) for t in range(nt))
        edge = lax.broadcasted_iota(jnp.int32, (metas, tile), 0)
        gb_rows = jnp.where(edge == 0, gb[:, :tile], jnp.where(edge == 1, gb[:, tile:], 0.0))
        wfin[l, pl.ds(2 * pad, metas), :] = gb_rows.astype(BF)
        wrecv[l] = wsend[l]
        products(l, precv, l)

        for t in range(nt):
            act_o[pl.ds(t * tile, tile), :] = flip(act_t[t])
        act_copy.start()

        each(L, lambda d: m_arrival(d).wait_recv(), 1)
        each(L, lambda d: m_copy(d).wait_send(), 1)
        each(2 * H, lambda i: y_copy(i).wait_send(), 2)
        pl.semaphore_wait(ready, L)

        w_all.wait_recv()
        total = wrecv[0].astype(F32)
        for p in range(1, L):
            total = total + wrecv[p].astype(F32)
        wfin[l, pl.ds(0, 2 * pad), :] = (total * grad_scale).astype(BF)

        def f_copy(d):
            return remote(wfin.at[l], wfin.at[l], f_send, f_recv, other(d), r)

        def e_copy(d):
            return remote(wfin.at[l], wfin.at[l], e_send, f_recv, d, twin)

        def give(i):
            e_copy(other(i)).start()
            f_copy(i).start()

        e_copy(l).start()
        each(L - 1, give)

        def add_products(ids):
            sums = [hid[pl.ds(c * fs, fs), :] for c in range(nt)]
            for p in ids:
                meta = mrecv[p].astype(F32)
                for k in range(slots):
                    part = precv[p, pl.ds(k * fs, fs), :].astype(F32)
                    for c in range(nt):
                        at = 2 * nt * k + nt + c
                        sums[c] = sums[c] + meta[at:at + 1, :] * part
            for c in range(nt):
                hid[pl.ds(c * fs, fs), :] = sums[c]

        def take_products(ds):
            for d in ds:
                q_arrival(d).wait_recv()
            add_products([nearest(d) for d in ds])

        add_products([l])
        groups(L - 1, 2, take_products)
        gft[h] = hid[...].astype(BF)
        each(H, lambda d: g_copy(d, lax.rem(twin + 2 * (H - 1 - d), R)).start())
        each(H, lambda d: g_copy(H - 1 + d, lax.rem(r + 2 * d, R)).start(), 1)

        act_copy.wait_send()
        each(L - 1, lambda i: q_copy(i).wait_send())
        w_all.wait_send()

        each(H, lambda d: g_arrival(lax.rem(h + d, H)).wait_recv(), 1)
        put_gf()
        f_some.wait_recv()
        put_gw()

        each(2 * H - 1, lambda d: g_copy(d, twin).wait_send())
        f_all.wait_send()
        f_some.wait_send()


def write_kernel(*refs):
    n = (len(refs) - 1) // 2
    copies = [pltpu.make_async_copy(refs[i], refs[n + i], refs[-1].at[i]) for i in range(n)]
    for copy in copies:
        copy.start()
    for copy in copies:
        copy.wait()


def write_out(*arrays):
    n = len(arrays)
    return pl.pallas_call(
        write_kernel,
        out_shape=tuple(jax.ShapeDtypeStruct(a.shape, a.dtype) for a in arrays),
        in_specs=[pl.BlockSpec(memory_space=pltpu.VMEM)] * n,
        out_specs=(pl.BlockSpec(memory_space=pltpu.HBM),) * n,
        scratch_shapes=[pltpu.SemaphoreType.DMA((n,))],
        name="write_out",
    )(*[pltpu.with_memory_space_constraint(a, pltpu.VMEM) for a in arrays])


def local(features, weight, out_bias, tile_values, tile_rows, tile_cols, tile_counts, cotangent):
    L, R = lax.axis_size("layer"), lax.axis_size("rep")
    H = R // 2
    rows_dev, hidden = cotangent.shape
    f_in = features.shape[1]
    _, sections, slots, tile, _ = tile_values.shape
    nt = rows_dev // tile
    fs = f_in // H
    metas = slots * 2 * nt
    pad = -(-(f_in // L) // 16) * 16
    vmem = pl.BlockSpec(memory_space=pltpu.VMEM)
    hbm = pl.BlockSpec(memory_space=pltpu.HBM)
    sem = pltpu.SemaphoreType.DMA
    regular = pltpu.SemaphoreType.REGULAR
    grad_scale = 1.0 / math.sqrt(rows_dev * L)
    act, gf, gw, gb = pl.pallas_call(
        functools.partial(kernel, L, R, grad_scale),
        out_shape=(
            jax.ShapeDtypeStruct((rows_dev, hidden), BF),
            jax.ShapeDtypeStruct((rows_dev, f_in), BF),
            jax.ShapeDtypeStruct((f_in, hidden), F32),
            jax.ShapeDtypeStruct((1, hidden), F32),
        ),
        in_specs=[hbm] * 8,
        out_specs=(vmem, vmem, vmem, vmem),
        scratch_shapes=[
            pltpu.VMEM(features.shape, BF),
            pltpu.VMEM(weight.shape, BF),
            pltpu.VMEM((1, hidden), F32),
            pltpu.SMEM(tile_rows.shape, jnp.int32),
            pltpu.SMEM(tile_rows.shape, jnp.int32),
            pltpu.SMEM(tile_rows.shape, jnp.int32),
            pltpu.VMEM(cotangent.shape, BF),
            sem((8,)),
            pltpu.VMEM((L, slots * tile + metas, tile), BF),
            pltpu.VMEM((L, nt * fs, tile), BF),
            pltpu.VMEM((H, nt * fs, tile), BF),
            pltpu.VMEM((hidden, f_in), BF),
            pltpu.VMEM((hidden, tile), F32),
            pltpu.VMEM((nt, hidden, tile), BF),
            pltpu.VMEM((nt, hidden, tile), BF),
            pltpu.VMEM((nt, hidden, tile), BF),
            pltpu.VMEM((nt * fs, tile), F32),
            pltpu.VMEM((L, slots * fs, tile), BF),
            pltpu.VMEM((L, slots * fs, tile), BF),
            pltpu.VMEM((L, metas, tile), BF),
            pltpu.VMEM((L, 2 * pad, tile), BF),
            pltpu.VMEM((L, 2 * pad, tile), BF),
            pltpu.VMEM((L, 2 * pad + metas, tile), BF),
            pltpu.VMEM((H, nt * fs, tile), BF),
            sem((H * sections,)), sem((L,)),
            sem((L,)), sem((L,)), sem((L,)),
            sem((2 * H,)), sem((2 * H,)),
            sem((L,)), sem((L,)),
            sem((L,)), sem((L,)),
            sem, sem,
            sem, sem, sem,
            sem((R,)), sem((H,)),
            sem, sem,
            regular, regular,
        ],
        compiler_params=pltpu.CompilerParams(
            collective_id=0, has_side_effects=True, vmem_limit_bytes=32 * 1024 * 1024
        ),
        name="graph_layer",
    )(*[pltpu.with_memory_space_constraint(x, pltpu.HBM) for x in (
        features, weight, out_bias.reshape(1, hidden),
        tile_values.reshape(sections, slots * tile, tile), tile_rows, tile_cols,
        tile_counts, cotangent)])
    return write_out(act, gf, gw, gb.reshape(hidden))


def solution(mesh):
    in_specs = (
        P("layer", None),
        P(),
        P(),
        P("layer", "rep", None, None, None),
        P("layer", "rep", None),
        P("layer", "rep", None),
        P("layer", "rep", None),
        P("layer", None),
    )
    out_specs = (P("layer", None), P("layer", None), P(), P())
    return jax.shard_map(local, mesh=mesh, in_specs=in_specs, out_specs=out_specs, check_vma=False)
```
